256 devices in a mesh: tm: 32 (over x, y, core), space: 8 (over z).
Axes of the slice: x: 4, y: 4, z: 8, core: 2. Of those that a mesh axis runs over, the one named last changes fastest.
Arguments:
- feats: bfloat16 [128, 32, 96, 256], P('tm', 'space'), may hold values from -120 to 120
- clip_ids: int32 [32], replicated, may hold values from 0 to 7, never falling along the last dimension, each value on 1 to 8 neighbouring positions
- gain_one: float32 [256], replicated, may hold values from 0.25 to 1.75
- shift_one: float32 [256], replicated, may hold values from -3 to 3
- kernel_one: bfloat16 [3, 3, 3, 256, 256], replicated, may hold values from -0.078125 to 0.078125
- gain_two: float32 [256], replicated, may hold values from 0.25 to 1.75
- shift_two: float32 [256], replicated, may hold values from -3 to 3
- kernel_two: bfloat16 [3, 3, 3, 256, 256], replicated, may hold values from -0.078125 to 0.078125
Outputs:
- block_out: float32 [128, 32, 96, 256], P('tm', 'space')
The draws below stay inside these ranges and needn't reach their ends.
Inputs may be any that keep to these rules, and one draw needn't show every extreme that they name: `clip_ids`: clip numbers of the slabs in order, never falling; every clip covers 1 to 8 consecutive slabs, at least one exactly 8.
All inputs are finite; a program needn't handle non-finite values.
Results may differ from the reference program's by a relative error of at most 0.0015.
Values may be sent and summed in bfloat16 or wider, within the bound.
A program may use at most 128 MiB of HBM per device.

```python
import math
import jax
import jax.numpy as jnp
import numpy as np
from jax import lax

C = 256
GROUPS = 32
FR = 4
COLS = 96
NFR = 128
NROWS = 32
CLIPS = 8
N_TM = 32


def draw_feats(key, part):
    key_base = jax.random.fold_in(key, 0)
    key_cell = jax.random.fold_in(key, 1)
    key_chan = jax.random.fold_in(key, 2)
    key_slab = jax.random.fold_in(key, 4)
    key_row = jax.random.fold_in(key, 5)
    shape = (NFR, NROWS, COLS, C)
    slab_total = NFR // FR
    slab_pos = jnp.arange(slab_total, dtype=jnp.float32) / max(slab_total - 1, 1)
    slab_amp = jnp.exp(slab_pos * math.log(3.0) + jax.random.uniform(key_slab, (slab_total,), jnp.float32, 0.0, math.log(4.0)))
    frame_amp = jnp.repeat(slab_amp, FR)[:, None, None, None]
    row_pos = jnp.arange(NROWS, dtype=jnp.float32) / max(NROWS - 1, 1)
    row_amp = jnp.exp(row_pos * math.log(3.0) + jax.random.uniform(key_row, (NROWS,), jnp.float32, 0.0, math.log(6.0)))[None, :, None, None]
    chan = jnp.exp(jax.random.uniform(key_chan, (C,), jnp.float32, -math.log(2.0), math.log(2.0)))
    base = jnp.clip(jax.random.normal(key_base, shape, jnp.float32), -6.0, 6.0)
    cell = jnp.exp(jax.random.uniform(key_cell, (NFR, NROWS, COLS, 1), jnp.float32) * math.log(10.0))
    values = 0.05 * frame_amp * row_amp * cell * chan * base
    return jnp.clip(values, -120.0, 120.0).astype(jnp.bfloat16)


def split_up(number_of, total, bound, lean):
    loads = [(1 << 20) // math.isqrt(grade ** lean) + 1 for grade in range(2, number_of + 1)]
    surplus, counts = total - bound - (number_of - 1), [1] * (number_of - 1)
    while surplus > 0:
        free = [i for i in range(number_of - 1) if counts[i] < bound]
        pool, budget = sum([loads[i] for i in free]), surplus
        for i in free:
            more = min(bound - counts[i], max(1, budget * loads[i] // pool), surplus)
            counts[i] = counts[i] + more
            surplus = surplus - more
    return np.array([bound] + counts)


def uneven(key, count, total, reach, lean):
    if count == 2:
        one = jax.random.randint(key, (), max(1, total - reach), min(reach, total - 1) + 1)
        return jnp.stack([one, total - one])
    sizes = jnp.asarray(split_up(count, total, reach, lean), jnp.int32)
    twos = (count - 1) // 2
    source_of, receiver = sizes[1:1 + 2 * twos:2], sizes[2:2 + 2 * twos:2]
    slack = jnp.minimum(source_of - 1, reach - receiver)
    passed = jax.random.randint(jax.random.fold_in(key, 1), (twos,), 0, 1 << 20) % (slack + 1)
    sizes = sizes.at[1:1 + 2 * twos:2].set(source_of - passed).at[2:2 + 2 * twos:2].set(receiver + passed)
    return sizes[jax.random.permutation(jax.random.fold_in(key, 2), count)]


def scatter_about(rng, extent, deviation, limit, held_as=jnp.bfloat16):
    result = jax.random.normal(rng, extent, jnp.float32) * deviation
    return jnp.minimum(jnp.maximum(result, -limit), limit).astype(held_as)


def setup_inputs(seed: int = 0) -> dict:
    splits = jax.random.split(jax.random.key(seed), 9)
    feats = draw_feats(jax.random.fold_in(splits[8], 71), 0)
    clip_ids = jnp.searchsorted(jnp.cumsum(uneven(splits[1], CLIPS, N_TM, 8, 2)), jnp.arange(N_TM), side="right").astype(jnp.int32)
    gain_one = jnp.clip(1.0 + 0.15 * jax.random.normal(splits[2], (C,), jnp.float32), 0.25, 1.75)
    shift_one = scatter_about(splits[3], (C,), 0.5, 3.0, jnp.float32)
    kernel_one = scatter_about(splits[4], (3, 3, 3, C, C), (27 * C) ** -0.5, 0.078125)
    gain_two = jnp.clip(1.0 + 0.15 * jax.random.normal(splits[5], (C,), jnp.float32), 0.25, 1.75)
    shift_two = scatter_about(splits[6], (C,), 0.5, 3.0, jnp.float32)
    kernel_two = scatter_about(splits[7], (3, 3, 3, C, C), (27 * C) ** -0.5, 0.078125)
    return {"feats": feats, "clip_ids": clip_ids, "gain_one": gain_one, "shift_one": shift_one, "kernel_one": kernel_one, "gain_two": gain_two, "shift_two": shift_two, "kernel_two": kernel_two}


def clip_norm(values, clip_frame, gain, shift):
    width = values.shape[3]
    grouped = values.reshape(NFR, -1, GROUPS, width // GROUPS)
    frame_sum = lax.optimization_barrier(jnp.sum(grouped, axis=(1, 3)))
    frame_square = lax.optimization_barrier(jnp.sum(grouped * grouped, axis=(1, 3)))
    member = (clip_frame[:, None] == jnp.arange(CLIPS, dtype=jnp.int32)[None, :]).astype(jnp.float32)
    clip_sum = jnp.dot(member.T, frame_sum, precision=lax.Precision.HIGHEST)
    clip_square = jnp.dot(member.T, frame_square, precision=lax.Precision.HIGHEST)
    per_sum = jnp.dot(member, clip_sum, precision=lax.Precision.HIGHEST)
    per_square = jnp.dot(member, clip_square, precision=lax.Precision.HIGHEST)
    frames_in = jnp.dot(member, lax.optimization_barrier(jnp.sum(member, axis=0)), precision=lax.Precision.HIGHEST)
    count = frames_in * (NROWS * COLS * (width // GROUPS))
    mean = per_sum / count[:, None]
    variance = per_square / count[:, None] - mean * mean
    scale = lax.rsqrt(variance + 1e-06)
    normed = (grouped - mean[:, None, :, None]) * scale[:, None, :, None]
    normed = normed.reshape(values.shape) * gain + shift
    return jax.nn.silu(normed).astype(jnp.bfloat16)

def causal_conv(act, kernel, start_frame):
    width = act.shape[3]
    frame_index = jnp.arange(NFR, dtype=jnp.int32)
    total = jnp.zeros((NFR * NROWS * COLS, kernel.shape[4]), jnp.float32)
    for tap_time in range(3):
        source = jnp.maximum(frame_index - 2 + tap_time, start_frame).astype(jnp.int32)
        taken = jnp.take(act, source, axis=0)
        padded = jnp.pad(taken, ((0, 0), (1, 1), (1, 1), (0, 0)), mode='edge')
        for tap_row in range(3):
            window = padded[:, tap_row:tap_row + NROWS]
            stacked = jnp.concatenate([window[:, :, offset:offset + COLS] for offset in range(3)], axis=3)
            stacked = stacked.reshape(-1, 3 * width)
            total = total + jnp.dot(stacked, kernel[tap_time, tap_row].reshape(3 * width, -1), preferred_element_type=jnp.float32)
    return total.reshape(NFR, NROWS, COLS, -1)

def reference(feats, clip_ids, gain_one, shift_one, kernel_one, gain_two, shift_two, kernel_two):
    slabs = jnp.arange(N_TM, dtype=jnp.int32)
    starts = jnp.concatenate([jnp.ones((1,), bool), clip_ids[1:] != clip_ids[:-1]])
    first_slab = lax.cummax(jnp.where(starts, slabs, 0).astype(jnp.int32), axis=0)
    slab_of = (jnp.arange(NFR, dtype=jnp.int32) // FR).astype(jnp.int32)
    start_frame = (jnp.take(first_slab, slab_of) * FR).astype(jnp.int32)
    clip_frame = jnp.take(clip_ids, slab_of).astype(jnp.int32)
    inputs = feats.astype(jnp.float32)
    first = clip_norm(inputs, clip_frame, gain_one, shift_one)
    hidden = causal_conv(first, kernel_one, start_frame).astype(jnp.bfloat16)
    second = clip_norm(hidden.astype(jnp.float32), clip_frame, gain_two, shift_two)
    return inputs + causal_conv(second, kernel_two, start_frame)
```

```python
import functools

import jax
import jax.numpy as jnp
from jax import lax
from jax.experimental import pallas as pl
from jax.experimental.pallas import tpu as pltpu
from jax.sharding import PartitionSpec as P

GROUPS = 32
REACH = 7
MESH = pl.DeviceIdType.MESH
F32 = jnp.float32
BF16 = jnp.bfloat16


def local_copy(src, dst, sem):
    return pltpu.make_async_copy(src, dst, sem)


def remote_copy(src, dst, send_sem, recv_sem, device):
    return pltpu.make_async_remote_copy(
        src_ref=src,
        dst_ref=dst,
        send_sem=send_sem,
        recv_sem=recv_sem,
        device_id=device,
        device_id_type=MESH,
    )


def wait_for(ref, sem):
    pltpu.make_async_copy(ref, ref, sem).wait()


def group_total(value, per_group):
    lane = lax.broadcasted_iota(jnp.int32, value.shape, 1)
    width = value.shape[1]
    step = 1
    while step < per_group:
        upper = pltpu.roll(value, step, 1)
        lower = pltpu.roll(value, width - step, 1)
        value = value + jnp.where((lane & step) != 0, upper, lower)
        step *= 2
    return value


def kernel(
    n_tm,
    n_space,
    feats,
    clip_ids,
    gain_one,
    shift_one,
    kernel_one,
    gain_two,
    shift_two,
    kernel_two,
    out,
    raw_one,
    raw_two,
    act,
    weights_one,
    weights_two,
    result,
    affine,
    ids,
    row_sums_one,
    row_sums_two,
    slab_sums_one,
    slab_sums_two,
    load_sem,
    weight_sem,
    affine_sem,
    ids_sem,
    out_sem,
    stat_send,
    stat_recv,
    halo_send,
    halo_recv,
):
    frames, rows, cols, width = feats.shape
    per_group = width // GROUPS
    slab = lax.axis_index("tm")
    place = lax.axis_index("space")
    after = lax.rem(slab + 1, n_tm)
    before = lax.rem(slab + n_tm - 1, n_tm)
    down = lax.rem(place + 1, n_space)
    up = lax.rem(place + n_space - 1, n_space)

    loads = [
        local_copy(feats.at[f], raw_one.at[f + 2, pl.ds(1, rows)], load_sem.at[f])
        for f in range(frames)
    ]
    for load in loads:
        load.start()

    barrier = pltpu.get_barrier_semaphore()

    def signal(tm, space):
        pl.semaphore_signal(barrier, inc=1, device_id=(tm, space), device_id_type=MESH)

    for k in range(1, n_space):
        signal(slab, lax.rem(place + k, n_space))
    for k in range(1, REACH + 1):
        signal(lax.rem(slab + k, n_tm), place)
        signal(lax.rem(slab + n_tm - k, n_tm), place)
    for tm in (after, before):
        for space in (up, down):
            signal(tm, space)

    ids_load = local_copy(clip_ids, ids, ids_sem)
    ids_load.start()
    affine_loads = [
        local_copy(ref, affine.at[i], affine_sem.at[i])
        for i, ref in enumerate((gain_one, shift_one, gain_two, shift_two))
    ]
    for load in affine_loads:
        load.start()
    weight_loads = [
        local_copy(kernel_one, weights_one, weight_sem.at[0]),
        local_copy(kernel_two, weights_two, weight_sem.at[1]),
    ]
    for load in weight_loads:
        load.start()

    def add_up(value, sums):
        total, square = sums
        value = value.reshape(-1, 8, width)
        return total + jnp.sum(value, axis=0), square + jnp.sum(value * value, axis=0)

    nothing = (jnp.zeros((8, width), F32), jnp.zeros((8, width), F32))

    def share_rows(sums, row_sums, which):
        total, square = sums
        row_sums[place, 0:1] = jnp.sum(total, axis=0, keepdims=True)
        row_sums[place, 1:2] = jnp.sum(square, axis=0, keepdims=True)
        copies = []
        for k in range(1, n_space):
            copy = remote_copy(
                row_sums.at[place],
                row_sums.at[place],
                stat_send.at[which, 0],
                stat_recv.at[which, 0],
                (slab, lax.rem(place + k, n_space)),
            )
            copy.start()

    def share_slabs(row_sums, slab_sums, which):
        wait_for(row_sums.at[pl.ds(0, n_space - 1)], stat_recv.at[which, 0])
        slab_sums[REACH] = jnp.sum(row_sums[...], axis=0)
        for k in range(1, REACH + 1):
            for offset in (k, -k):
                remote_copy(
                    slab_sums.at[REACH],
                    slab_sums.at[REACH - offset],
                    stat_send.at[which, 1],
                    stat_recv.at[which, 1],
                    (lax.rem(slab + n_tm + offset, n_tm), place),
                ).start()

    def clip_stats(slab_sums, which, own, members):
        wait_for(slab_sums.at[pl.ds(0, 2 * REACH)], stat_recv.at[which, 1])
        total = jnp.zeros((2, width), F32)
        for k in range(2 * REACH + 1):
            total = total + slab_sums[k] * members[k]
        total = group_total(total, per_group)
        slabs_in = functools.reduce(lambda a, b: a + b, members)
        count = slabs_in * float(frames * rows * n_space * cols * per_group)
        total = total / jnp.full((2, width), count, F32)
        mean = total[0:1]
        variance = total[1:2] - mean * mean
        return mean, lax.rsqrt(variance + 1e-06)

    def send_halo(raw, stage, first, count, ahead):
        span = pl.ds(first, count)
        copies = [
            ((span, pl.ds(1, 1)), (span, pl.ds(rows + 1, 1)), (slab, up)),
            ((span, pl.ds(rows, 1)), (span, pl.ds(0, 1)), (slab, down)),
        ]
        if ahead:
            last = pl.ds(frames, 2)
            front = pl.ds(0, 2)
            copies += [
                ((last, pl.ds(1, rows)), (front, pl.ds(1, rows)), (after, place)),
                ((last, pl.ds(1, 1)), (front, pl.ds(rows + 1, 1)), (after, up)),
                ((last, pl.ds(rows, 1)), (front, pl.ds(0, 1)), (after, down)),
            ]
        made = []
        for i, (src, dst, device) in enumerate(copies):
            made.append(
                remote_copy(
                    raw.at[src],
                    raw.at[dst],
                    halo_send.at[stage, i],
                    halo_recv.at[stage, i],
                    device,
                )
            )
        return made

    sums = nothing
    for f in range(frames):
        loads[f].wait()
        for r in range(rows):
            sums = add_up(raw_one[f + 2, r + 1].astype(F32), sums)
    pl.semaphore_wait(barrier, (n_space - 1) + 2 * REACH + 4)
    share_rows(sums, row_sums_one, 0)
    halo_one = send_halo(raw_one, 0, 2, frames, True)
    for copy in halo_one:
        copy.start()

    ids_load.wait()
    own = ids[slab]
    members = [
        jnp.where(ids[lax.rem(slab + n_tm + k - REACH, n_tm)] == own, 1.0, 0.0).astype(F32)
        for k in range(2 * REACH + 1)
    ]
    starting = jnp.logical_or(slab == 0, ids[before] != own)
    fresh = jnp.full((cols, width), jnp.where(starting, 1, 0), jnp.int32) != 0
    top = jnp.where(place == 0, 1, 0)
    bottom = jnp.where(place == n_space - 1, rows, rows + 1)

    share_slabs(row_sums_one, slab_sums_one, 0)
    for load in affine_loads:
        load.wait()
    mean, scale = clip_stats(slab_sums_one, 0, own, members)

    def normed(value, mean, factor, shift):
        value = (value - mean) * factor + shift
        return (value / (1.0 + jnp.exp(-value))).astype(BF16)

    def norm_rows(raw, mean, factor, shift, first, count, which_rows):
        def step(f, carry):
            for r in which_rows:
                source = top if r == 0 else bottom if r == rows + 1 else r
                act[f, r] = normed(raw[f, source].astype(F32), mean, factor, shift)
            return carry

        lax.fori_loop(first, first + count, step, 0)

    def norm_front(raw, mean, factor, shift):
        def step(r, carry):
            source = jnp.minimum(jnp.maximum(r, top), bottom)
            opening = raw[2, source].astype(F32)
            for f in range(2):
                value = jnp.where(fresh, opening, raw[f, source].astype(F32))
                act[f, r] = normed(value, mean, factor, shift)
            return carry

        lax.fori_loop(0, rows + 2, step, 0)

    def conv(f, weights):
        size = rows * cols
        taps = [(i, j) for i in range(3) for j in range(3)]
        left = jnp.concatenate(
            [act[f + i, pl.ds(j, rows)].reshape(size, width) for i, j in taps], axis=1
        )
        parts = []
        for l in range(3):
            right = jnp.concatenate([weights[i, j, l] for i, j in taps], axis=0)
            parts.append(jnp.dot(left, right, preferred_element_type=F32))
        col = lax.rem(lax.broadcasted_iota(jnp.int32, (size, width), 0), cols)
        earlier = jnp.where(col == 0, parts[0], pltpu.roll(parts[0], 1, 0))
        later = jnp.where(col == cols - 1, parts[2], pltpu.roll(parts[2], size - 1, 0))
        return parts[1] + earlier + later

    inner = tuple(range(1, rows + 1))
    outer = (0, rows + 1)

    factor = scale * affine[0]
    shift = affine[1]
    norm_rows(raw_one, mean, factor, shift, 2, frames, inner)
    for copy in halo_one[:2]:
        copy.wait_recv()
    norm_rows(raw_one, mean, factor, shift, 2, frames, outer)
    weight_loads[0].wait()

    def conv_one(f, sums):
        hidden = conv(f, weights_one).astype(BF16)
        raw_two[f + 2, pl.ds(1, rows)] = hidden.reshape(rows, cols, width)
        return add_up(hidden.astype(F32), sums)

    sums = lax.fori_loop(frames - 2, frames, conv_one, nothing)
    halo_two = send_halo(raw_two, 1, frames, 2, True)
    for copy in halo_two:
        copy.start()
    for copy in halo_one[2:]:
        copy.wait_recv()
    norm_front(raw_one, mean, factor, shift)
    sums = lax.fori_loop(0, frames - 2, conv_one, sums)

    share_rows(sums, row_sums_two, 1)
    halo_three = send_halo(raw_two, 2, 2, frames - 2, False)
    for copy in halo_three:
        copy.start()
    share_slabs(row_sums_two, slab_sums_two, 1)
    mean, scale = clip_stats(slab_sums_two, 1, own, members)
    factor = scale * affine[2]
    shift = affine[3]
    norm_rows(raw_two, mean, factor, shift, 2, frames, inner)
    for copy in halo_two[:2] + halo_three:
        copy.wait_recv()
    norm_rows(raw_two, mean, factor, shift, 2, frames, outer)
    weight_loads[1].wait()

    def conv_two(f, carry):
        value = conv(f, weights_two).reshape(rows, cols, width)
        result[f] = value + raw_one[f + 2, pl.ds(1, rows)].astype(F32)
        return carry

    def store(half):
        span = pl.ds(half * 2, 2)
        return local_copy(result.at[span], out.at[span], out_sem.at[half])

    lax.fori_loop(frames - 2, frames, conv_two, 0)
    store(1).start()
    for copy in halo_two[2:]:
        copy.wait_recv()
    norm_front(raw_two, mean, factor, shift)
    lax.fori_loop(0, frames - 2, conv_two, 0)
    store(0).start()

    for copy in halo_one + halo_two + halo_three:
        copy.wait_send()
    for which, row_sums, slab_sums in (
        (0, row_sums_one, slab_sums_one),
        (1, row_sums_two, slab_sums_two),
    ):
        wait_for(row_sums.at[pl.ds(0, n_space - 1)], stat_send.at[which, 0])
        wait_for(slab_sums.at[pl.ds(0, 2 * REACH)], stat_send.at[which, 1])
    store(1).wait()
    store(0).wait()


def solution(mesh):
    n_tm, n_space = mesh.shape["tm"], mesh.shape["space"]

    def on_device(
        feats, clip_ids, gain_one, shift_one, kernel_one, gain_two, shift_two, kernel_two
    ):
        frames, rows, cols, width = feats.shape
        extended = (frames + 2, rows + 2, cols, width)
        vmem = pltpu.VMEM
        dma = pltpu.SemaphoreType.DMA
        row = lambda value: value.reshape(1, width)
        return pl.pallas_call(
            functools.partial(kernel, n_tm, n_space),
            out_shape=jax.ShapeDtypeStruct(feats.shape, F32),
            in_specs=[pl.BlockSpec(memory_space=pltpu.HBM)] * 8,
            out_specs=pl.BlockSpec(memory_space=pltpu.HBM),
            scratch_shapes=[
                vmem(extended, BF16),
                vmem(extended, BF16),
                vmem(extended, BF16),
                vmem(kernel_one.shape, BF16),
                vmem(kernel_two.shape, BF16),
                vmem(feats.shape, F32),
                vmem((4, 1, width), F32),
                pltpu.SMEM((n_tm,), jnp.int32),
                vmem((n_space, 2, width), F32),
                vmem((n_space, 2, width), F32),
                vmem((2 * REACH + 1, 2, width), F32),
                vmem((2 * REACH + 1, 2, width), F32),
                dma((frames,)),
                dma((2,)),
                dma((4,)),
                dma,
                dma((2,)),
                dma((2, 2)),
                dma((2, 2)),
                dma((3, 5)),
                dma((3, 5)),
            ],
            compiler_params=pltpu.CompilerParams(
                collective_id=0, has_side_effects=True, vmem_limit_bytes=60 << 20
            ),
            cost_estimate=pl.CostEstimate(
                flops=2 * 2 * 27 * frames * rows * cols * width * width,
                bytes_accessed=12 << 20,
                transcendentals=0,
            ),
            name="residual_block",
        )(
            feats,
            clip_ids,
            row(gain_one),
            row(shift_one),
            kernel_one,
            row(gain_two),
            row(shift_two),
            kernel_two,
        )

    return jax.shard_map(
        on_device,
        mesh=mesh,
        in_specs=(P("tm", "space", None, None), P(), P(), P(), P(), P(), P(), P()),
        out_specs=P("tm", "space", None, None),
        check_vma=False,
    )
```

```python
import functools

import jax
import jax.numpy as jnp
from jax import lax
from jax.experimental import pallas as pl
from jax.experimental.pallas import tpu as pltpu
from jax.sharding import PartitionSpec as P

GROUPS = 32
REACH = 7
WINDOW = 2 * REACH + 1
LANES = 128
MESH = pl.DeviceIdType.MESH
F32 = jnp.float32
BF16 = jnp.bfloat16


def local_copy(src, dst, sem):
    return pltpu.make_async_copy(src, dst, sem)


def remote_copy(src, dst, send_sem, recv_sem, device):
    return pltpu.make_async_remote_copy(
        src_ref=src,
        dst_ref=dst,
        send_sem=send_sem,
        recv_sem=recv_sem,
        device_id=device,
        device_id_type=MESH,
    )


def wait_for(ref, sem):
    pltpu.make_async_copy(ref, ref, sem).wait()


def group_total(value, per_group):
    lane = lax.broadcasted_iota(jnp.int32, value.shape, 1)
    width = value.shape[1]
    step = 1
    while step < per_group:
        upper = pltpu.roll(value, step, 1)
        lower = pltpu.roll(value, width - step, 1)
        value = value + jnp.where((lane & step) != 0, upper, lower)
        step *= 2
    return value


def add_up(value, sums):
    total, square = sums
    value = value.reshape(-1, 8, value.shape[-1])
    return total + jnp.sum(value, axis=0), square + jnp.sum(value * value, axis=0)


def pack_sums(sums, per_group):
    total, square = (jnp.sum(s, axis=0, keepdims=True) for s in sums)
    parts = [
        total[:, :LANES],
        square[:, :LANES],
        total[:, LANES:],
        square[:, LANES:],
    ]
    parts = group_total(jnp.concatenate(parts, axis=0), per_group)
    kind = lax.broadcasted_iota(jnp.int32, (1, LANES), 1) & 3
    packed = parts[3:4]
    for i in range(3):
        packed = jnp.where(kind == i, parts[i : i + 1], packed)
    return packed


def unpack_stats(packed, count, per_group):
    shape = (4, LANES)
    row = lax.broadcasted_iota(jnp.int32, shape, 0)
    lane = lax.broadcasted_iota(jnp.int32, shape, 1)
    spread = jnp.where((lane & (per_group - 1)) == row, jnp.broadcast_to(packed, shape), 0.0)
    total = group_total(spread, per_group) / jnp.full(shape, count, F32)
    mean = jnp.concatenate([total[0:1], total[2:3]], axis=1)
    variance = jnp.concatenate([total[1:2], total[3:4]], axis=1) - mean * mean
    return mean, lax.rsqrt(variance + 1e-06)


def row_limits(place, n_space, rows):
    top = jnp.where(place == 0, 1, 0)
    bottom = jnp.where(place == n_space - 1, rows, rows + 1)
    return top, bottom


def normed(value, mean, factor, shift):
    value = (value - mean) * factor + shift
    return (value / (1.0 + jnp.exp(-value))).astype(BF16)


def norm_frame(raw, act, f, limits, fresh, stats):
    rows = raw.shape[1] - 2
    top, bottom = limits
    for r in range(rows + 2):
        source = top if r == 0 else bottom if r == rows + 1 else r
        value = raw[f, source].astype(F32)
        if f < 2:
            value = jnp.where(fresh, raw[2, source].astype(F32), value)
        act[f, r] = normed(value, *stats)


def conv(act, weights, f, count):
    rows, cols, width = act.shape[1] - 2, act.shape[2], act.shape[3]
    size = count * rows * cols
    parts = []
    for l in range(3):
        total = None
        for i in range(3):
            for j in range(3):
                left = act[f + i : f + i + count, j : j + rows].reshape(size, width)
                term = jnp.dot(left, weights[i, j, l], preferred_element_type=F32)
                total = term if total is None else total + term
        parts.append(total)
    col = lax.rem(lax.broadcasted_iota(jnp.int32, (size, width), 0), cols)
    earlier = jnp.where(col == 0, parts[0], pltpu.roll(parts[0], 1, 0))
    later = jnp.where(col == cols - 1, parts[2], pltpu.roll(parts[2], size - 1, 0))
    return parts[1] + earlier + later


def far_first(n_space):
    chips = (0.0, 1.0, 2.0, 1.7, 1.0)

    def hops(pair):
        return min(pair[1], n_space - pair[1]) + chips[(abs(pair[0]) + 1) // 2]

    pairs = [(k, d) for k in range(-REACH, REACH + 1) for d in range(n_space) if (k, d) != (0, 0)]
    return sorted(pairs, key=hops, reverse=True)


def front_kernel(
    n_tm,
    n_space,
    feats,
    clip_ids,
    gain_one,
    shift_one,
    kernel_one,
    gain_two,
    shift_two,
    kernel_two,
    raw_two,
    weights_two,
    table,
    raw_one,
    act,
    weights_one,
    affine,
    ids,
    row_sums,
    slab_sums,
    all_sums,
    load_sem,
    weight_sem,
    affine_sem,
    ids_sem,
    stat_send,
    stat_recv,
    halo_send,
    halo_recv,
):
    frames, rows, cols, width = feats.shape
    per_group = width // GROUPS
    slab = lax.axis_index("tm")
    place = lax.axis_index("space")
    after = lax.rem(slab + 1, n_tm)
    before = lax.rem(slab + n_tm - 1, n_tm)
    down = lax.rem(place + 1, n_space)
    up = lax.rem(place + n_space - 1, n_space)

    loads = [
        local_copy(feats.at[f], raw_one.at[f + 2, pl.ds(1, rows)], load_sem.at[f])
        for f in range(frames)
    ]
    for load in loads:
        load.start()

    barrier = pltpu.get_barrier_semaphore()

    def signal(tm, space):
        pl.semaphore_signal(barrier, inc=1, device_id=(tm, space), device_id_type=MESH)

    for k in range(1, n_space):
        signal(slab, lax.rem(place + k, n_space))
    for k in range(1, REACH + 1):
        signal(lax.rem(slab + k, n_tm), place)
        signal(lax.rem(slab + n_tm - k, n_tm), place)
    for tm in (after, before):
        for space in (up, down):
            signal(tm, space)

    ids_load = local_copy(clip_ids, ids, ids_sem)
    ids_load.start()
    affine_loads = [
        local_copy(ref, affine.at[i], affine_sem.at[i])
        for i, ref in enumerate((gain_one, shift_one, gain_two, shift_two))
    ]
    for load in affine_loads:
        load.start()
    weight_loads = [
        local_copy(kernel_one, weights_one, weight_sem.at[0]),
        local_copy(kernel_two, weights_two, weight_sem.at[1]),
    ]
    for load in weight_loads:
        load.start()

    def send_halo(raw, stage, first, count, ahead):
        span = pl.ds(first, count)
        copies = [
            ((span, pl.ds(1, 1)), (span, pl.ds(rows + 1, 1)), (slab, up)),
            ((span, pl.ds(rows, 1)), (span, pl.ds(0, 1)), (slab, down)),
        ]
        if ahead:
            last = pl.ds(frames, 2)
            front = pl.ds(0, 2)
            copies += [
                ((last, pl.ds(1, rows)), (front, pl.ds(1, rows)), (after, place)),
                ((last, pl.ds(1, 1)), (front, pl.ds(rows + 1, 1)), (after, up)),
                ((last, pl.ds(rows, 1)), (front, pl.ds(0, 1)), (after, down)),
            ]
        made = []
        for i, (src, dst, device) in enumerate(copies):
            made.append(
                remote_copy(
                    raw.at[src],
                    raw.at[dst],
                    halo_send.at[stage, i],
                    halo_recv.at[stage, i],
                    device,
                )
            )
        for copy in made:
            copy.start()
        return made

    nothing = (jnp.zeros((8, width), F32), jnp.zeros((8, width), F32))
    frame_count = float(frames * rows * n_space * cols * per_group)

    sums = nothing
    for f in range(frames):
        loads[f].wait()
        for r in range(rows):
            sums = add_up(raw_one[f + 2, r + 1].astype(F32), sums)
    row_sums[place] = pack_sums(sums, per_group)
    pl.semaphore_wait(barrier, (n_space - 1) + 2 * REACH + 4)
    for k in range(1, n_space):
        remote_copy(
            row_sums.at[place],
            row_sums.at[place],
            stat_send.at[0],
            stat_recv.at[0],
            (slab, lax.rem(place + k, n_space)),
        ).start()
    halo_one = send_halo(raw_one, 0, 2, frames, True)

    ids_load.wait()
    own = ids[slab]
    members = [
        jnp.where(ids[lax.rem(slab + n_tm + k - REACH, n_tm)] == own, 1.0, 0.0).astype(F32)
        for k in range(WINDOW)
    ]
    count = functools.reduce(lambda a, b: a + b, members) * frame_count
    starting = jnp.logical_or(slab == 0, ids[before] != own)
    starts = jnp.where(starting, 1.0, 0.0).astype(F32)
    fresh = jnp.full((cols, width), starts, F32) > 0.5
    limits = row_limits(place, n_space, rows)

    wait_for(row_sums.at[pl.ds(0, n_space - 1)], stat_recv.at[0])
    slab_sums[REACH] = jnp.sum(row_sums[...], axis=0)
    for k in range(REACH, 0, -1):
        for offset in (k, -k):
            remote_copy(
                slab_sums.at[REACH],
                slab_sums.at[REACH - offset],
                stat_send.at[1],
                stat_recv.at[1],
                (lax.rem(slab + n_tm + offset, n_tm), place),
            ).start()
    for load in affine_loads:
        load.wait()
    weight_loads[0].wait()
    for copy in halo_one:
        copy.wait_recv()
    wait_for(slab_sums.at[pl.ds(0, WINDOW - 1)], stat_recv.at[1])
    total = jnp.zeros((1, LANES), F32)
    for k in range(WINDOW):
        total = total + slab_sums[k] * members[k]
    mean, scale = unpack_stats(total, count, per_group)
    stats = (mean, scale * affine[0], affine[1])

    def conv_one(f, sums):
        hidden = conv(act, weights_one, f, 2).astype(BF16)
        raw_two[f + 2 : f + 4, 1 : rows + 1] = hidden.reshape(2, rows, cols, width)
        return add_up(hidden.astype(F32), sums)

    for f in (2, 3, 4, 5, 0, 1):
        norm_frame(raw_one, act, f, limits, fresh, stats)
    sums = conv_one(2, nothing)
    halo_two = send_halo(raw_two, 1, 4, 2, True)
    sums = conv_one(0, sums)

    all_sums[REACH * n_space + place] = pack_sums(sums, per_group)
    for offset, turn in far_first(n_space):
        remote_copy(
            all_sums.at[REACH * n_space + place],
            all_sums.at[(REACH - offset) * n_space + place],
            stat_send.at[2],
            stat_recv.at[2],
            (lax.rem(slab + n_tm + offset, n_tm), lax.rem(place + turn, n_space)),
        ).start()
    halo_three = send_halo(raw_two, 2, 2, 2, False)
    table[3:4] = jnp.full((1, width), starts, F32)
    table[2:3] = affine[3]
    weight_loads[1].wait()
    for copy in halo_two + halo_three:
        copy.wait_recv()
    for copy in halo_one + halo_two + halo_three:
        copy.wait_send()
    wait_for(row_sums.at[pl.ds(0, n_space - 1)], stat_send.at[0])
    wait_for(slab_sums.at[pl.ds(0, WINDOW - 1)], stat_send.at[1])
    others = all_sums.at[pl.ds(0, WINDOW * n_space - 1)]
    wait_for(others, stat_send.at[2])
    wait_for(others, stat_recv.at[2])
    total = jnp.zeros((1, LANES), F32)
    for k in range(WINDOW):
        total = total + jnp.sum(all_sums[pl.ds(k * n_space, n_space)], axis=0) * members[k]
    mean, scale = unpack_stats(total, count, per_group)
    table[0:1] = mean
    table[1:2] = scale * affine[2]


def back_kernel(n_space, feats, raw, weights, table, out, act, result, base, load_sem, out_sem):
    frames, rows, cols, width = feats.shape
    load = local_copy(feats, base, load_sem)
    load.start()
    limits = row_limits(lax.axis_index("space"), n_space, rows)
    stats = (table[0:1], table[1:2], table[2:3])
    fresh = jnp.broadcast_to(table[3:4], (cols, width)) > 0.5
    load.wait()

    def conv_two(f):
        value = conv(act, weights, f, 2).reshape(2, rows, cols, width)
        result[f : f + 2] = value + base[f : f + 2].astype(F32)

    def store(half):
        span = pl.ds(half * 2, 2)
        return local_copy(result.at[span], out.at[span], out_sem.at[half])

    for f in (2, 3, 4, 5, 0, 1):
        norm_frame(raw, act, f, limits, fresh, stats)
    conv_two(2)
    store(1).start()
    conv_two(0)
    store(0).start()
    store(1).wait()
    store(0).wait()


def solution(mesh):
    n_tm, n_space = mesh.shape["tm"], mesh.shape["space"]

    def on_device(
        feats, clip_ids, gain_one, shift_one, kernel_one, gain_two, shift_two, kernel_two
    ):
        frames, rows, cols, width = feats.shape
        extended = (frames + 2, rows + 2, cols, width)
        vmem = pltpu.VMEM
        dma = pltpu.SemaphoreType.DMA
        in_hbm = pl.BlockSpec(memory_space=pltpu.HBM)
        in_vmem = pl.BlockSpec(memory_space=pltpu.VMEM)
        row = lambda value: value.reshape(1, width)
        flops = 2 * 27 * frames * rows * cols * width * width
        raw_two, weights_two, table = pl.pallas_call(
            functools.partial(front_kernel, n_tm, n_space),
            out_shape=(
                vmem(extended, BF16),
                vmem(kernel_two.shape, BF16),
                vmem((8, width), F32),
            ),
            in_specs=[in_hbm] * 8,
            out_specs=[in_vmem] * 3,
            scratch_shapes=[
                vmem(extended, BF16),
                vmem(extended, BF16),
                vmem(kernel_one.shape, BF16),
                vmem((4, 1, width), F32),
                pltpu.SMEM((n_tm,), jnp.int32),
                vmem((n_space, 1, LANES), F32),
                vmem((WINDOW, 1, LANES), F32),
                vmem((WINDOW * n_space, 1, LANES), F32),
                dma((frames,)),
                dma((2,)),
                dma((4,)),
                dma,
                dma((3,)),
                dma((3,)),
                dma((3, 5)),
                dma((3, 5)),
            ],
            compiler_params=pltpu.CompilerParams(
                collective_id=0, has_side_effects=True, vmem_limit_bytes=54 << 20
            ),
            cost_estimate=pl.CostEstimate(
                flops=flops, bytes_accessed=8 << 20, transcendentals=0
            ),
            name="front",
        )(
            feats,
            clip_ids,
            row(gain_one),
            row(shift_one),
            kernel_one,
            row(gain_two),
            row(shift_two),
            kernel_two,
        )
        return pl.pallas_call(
            functools.partial(back_kernel, n_space),
            out_shape=jax.ShapeDtypeStruct(feats.shape, F32),
            in_specs=[in_hbm, in_vmem, in_vmem, in_vmem],
            out_specs=in_hbm,
            scratch_shapes=[
                vmem(extended, BF16),
                vmem(feats.shape, F32),
                vmem(feats.shape, BF16),
                dma,
                dma((2,)),
            ],
            compiler_params=pltpu.CompilerParams(vmem_limit_bytes=24 << 20),
            cost_estimate=pl.CostEstimate(
                flops=flops, bytes_accessed=3 << 20, transcendentals=0
            ),
            name="back",
        )(feats, raw_two, weights_two, table)

    return jax.shard_map(
        on_device,
        mesh=mesh,
        in_specs=(P("tm", "space", None, None), P(), P(), P(), P(), P(), P(), P()),
        out_specs=P("tm", "space", None, None),
        check_vma=False,
    )
```

```python
import functools

import jax
import jax.numpy as jnp
from jax import lax
from jax.experimental import pallas as pl
from jax.experimental.pallas import tpu as pltpu
from jax.sharding import PartitionSpec as P

GROUPS = 32
REACH = 7
WINDOW = 2 * REACH + 1
LANES = 128
MESH = pl.DeviceIdType.MESH
F32 = jnp.float32
BF16 = jnp.bfloat16


def local_copy(src, dst, sem):
    return pltpu.make_async_copy(src, dst, sem)


def remote_copy(src, dst, send_sem, recv_sem, device):
    return pltpu.make_async_remote_copy(
        src_ref=src,
        dst_ref=dst,
        send_sem=send_sem,
        recv_sem=recv_sem,
        device_id=device,
        device_id_type=MESH,
    )


def wait_for(ref, sem):
    pltpu.make_async_copy(ref, ref, sem).wait()


def group_total(value, per_group):
    lane = lax.broadcasted_iota(jnp.int32, value.shape, 1)
    width = value.shape[1]
    step = 1
    while step < per_group:
        upper = pltpu.roll(value, step, 1)
        lower = pltpu.roll(value, width - step, 1)
        value = value + jnp.where((lane & step) != 0, upper, lower)
        step *= 2
    return value


def add_up(value, sums):
    total, square = sums
    value = value.reshape(-1, 8, value.shape[-1])
    return total + jnp.sum(value, axis=0), square + jnp.sum(value * value, axis=0)


def pack_sums(sums, per_group):
    total, square = (jnp.sum(s, axis=0, keepdims=True) for s in sums)
    parts = [
        total[:, :LANES],
        square[:, :LANES],
        total[:, LANES:],
        square[:, LANES:],
    ]
    parts = group_total(jnp.concatenate(parts, axis=0), per_group)
    kind = lax.broadcasted_iota(jnp.int32, (1, LANES), 1) & 3
    packed = parts[3:4]
    for i in range(3):
        packed = jnp.where(kind == i, parts[i : i + 1], packed)
    return packed


def unpack_stats(packed, count, per_group):
    shape = (4, LANES)
    row = lax.broadcasted_iota(jnp.int32, shape, 0)
    lane = lax.broadcasted_iota(jnp.int32, shape, 1)
    spread = jnp.where((lane & (per_group - 1)) == row, jnp.broadcast_to(packed, shape), 0.0)
    total = group_total(spread, per_group) / jnp.full(shape, count, F32)
    mean = jnp.concatenate([total[0:1], total[2:3]], axis=1)
    variance = jnp.concatenate([total[1:2], total[3:4]], axis=1) - mean * mean
    return mean, lax.rsqrt(variance + 1e-06)


def row_limits(place, n_space, rows):
    top = jnp.where(place == 0, 1, 0)
    bottom = jnp.where(place == n_space - 1, rows, rows + 1)
    return top, bottom


def normed(value, mean, factor, shift):
    value = (value - mean) * factor + shift
    return (value / (1.0 + jnp.exp(-value))).astype(BF16)


def norm_frame(raw, act, f, limits, fresh, stats):
    rows = raw.shape[1] - 2
    top, bottom = limits
    for r in range(rows + 2):
        source = top if r == 0 else bottom if r == rows + 1 else r
        value = raw[f, source].astype(F32)
        if f < 2:
            value = jnp.where(fresh, raw[2, source].astype(F32), value)
        act[f, r] = normed(value, *stats)


def tap_sum(act, weights, f, count, l):
    rows, cols, width = act.shape[1] - 2, act.shape[2], act.shape[3]
    total = None
    for i in range(3):
        for j in range(3):
            left = act[f + i : f + i + count, j : j + rows].reshape(count * rows * cols, width)
            term = jnp.dot(left, weights[i, j, l], preferred_element_type=F32)
            total = term if total is None else total + term
    return total


def joined(parts, cols):
    size = parts[0].shape[0]
    col = lax.rem(lax.broadcasted_iota(jnp.int32, parts[0].shape, 0), cols)
    earlier = jnp.where(col == 0, parts[0], pltpu.roll(parts[0], 1, 0))
    later = jnp.where(col == cols - 1, parts[1], pltpu.roll(parts[1], size - 1, 0))
    return parts[2] + (earlier + later)


def conv_tiles(act, weights, tiles, finish):
    cols = act.shape[2]
    waiting = None
    for f, count in tiles:
        parts = [tap_sum(act, weights, f, count, 0)]
        if waiting is not None:
            finish(waiting[0], joined(waiting[1], cols))
        parts += [tap_sum(act, weights, f, count, l) for l in (2, 1)]
        waiting = (f, parts)
    finish(waiting[0], joined(waiting[1], cols))


def far_first(n_space):
    chips = (0.0, 1.0, 2.0, 1.7, 1.0)

    def hops(pair):
        return min(pair[1], n_space - pair[1]) + chips[(abs(pair[0]) + 1) // 2]

    pairs = [(k, d) for k in range(-REACH, REACH + 1) for d in range(n_space) if (k, d) != (0, 0)]
    return sorted(pairs, key=hops, reverse=True)


def front_kernel(
    n_tm,
    n_space,
    feats,
    clip_ids,
    gain_one,
    shift_one,
    kernel_one,
    gain_two,
    shift_two,
    kernel_two,
    raw_two,
    weights_two,
    table,
    raw_one,
    act,
    weights_one,
    affine,
    ids,
    row_sums,
    slab_sums,
    all_sums,
    load_sem,
    weight_sem,
    affine_sem,
    ids_sem,
    stat_send,
    stat_recv,
    halo_send,
    halo_recv,
):
    frames, rows, cols, width = feats.shape
    per_group = width // GROUPS
    slab = lax.axis_index("tm")
    place = lax.axis_index("space")
    after = lax.rem(slab + 1, n_tm)
    before = lax.rem(slab + n_tm - 1, n_tm)
    down = lax.rem(place + 1, n_space)
    up = lax.rem(place + n_space - 1, n_space)

    loads = [
        local_copy(feats.at[f], raw_one.at[f + 2, pl.ds(1, rows)], load_sem.at[f])
        for f in range(frames)
    ]
    for load in loads:
        load.start()

    barrier = pltpu.get_barrier_semaphore()

    def signal(tm, space):
        pl.semaphore_signal(barrier, inc=1, device_id=(tm, space), device_id_type=MESH)

    for k in range(1, n_space):
        signal(slab, lax.rem(place + k, n_space))
    for k in range(1, REACH + 1):
        signal(lax.rem(slab + k, n_tm), place)
        signal(lax.rem(slab + n_tm - k, n_tm), place)
    for tm in (after, before):
        for space in (up, down):
            signal(tm, space)

    ids_load = local_copy(clip_ids, ids, ids_sem)
    ids_load.start()
    affine_loads = [
        local_copy(ref, affine.at[i], affine_sem.at[i])
        for i, ref in enumerate((gain_one, shift_one, gain_two, shift_two))
    ]
    for load in affine_loads:
        load.start()
    weight_loads = [
        local_copy(kernel_one, weights_one, weight_sem.at[0]),
        local_copy(kernel_two, weights_two, weight_sem.at[1]),
    ]
    for load in weight_loads:
        load.start()

    def send_halo(raw, stage, first, count, ahead, corners):
        span = pl.ds(first, count)
        copies = [
            ((span, pl.ds(1, 1)), (span, pl.ds(rows + 1, 1)), (slab, up)),
            ((span, pl.ds(rows, 1)), (span, pl.ds(0, 1)), (slab, down)),
        ]
        last = pl.ds(frames, 2)
        front = pl.ds(0, 2)
        if ahead:
            copies += [((last, pl.ds(1, rows)), (front, pl.ds(1, rows)), (after, place))]
        if corners:
            copies += [
                ((last, pl.ds(1, 1)), (front, pl.ds(rows + 1, 1)), (after, up)),
                ((last, pl.ds(rows, 1)), (front, pl.ds(0, 1)), (after, down)),
            ]
        return start_copies(raw, stage, copies)

    def start_copies(raw, stage, copies):
        made = []
        for i, (src, dst, device) in enumerate(copies):
            made.append(
                remote_copy(
                    raw.at[src],
                    raw.at[dst],
                    halo_send.at[stage, i],
                    halo_recv.at[stage, i],
                    device,
                )
            )
        for copy in made:
            copy.start()
        return made

    nothing = (jnp.zeros((8, width), F32), jnp.zeros((8, width), F32))
    frame_count = float(frames * rows * n_space * cols * per_group)

    sums = nothing
    for f in range(frames):
        loads[f].wait()
        for r in range(rows):
            sums = add_up(raw_one[f + 2, r + 1].astype(F32), sums)
    row_sums[place] = pack_sums(sums, per_group)
    pl.semaphore_wait(barrier, (n_space - 1) + 2 * REACH + 4)
    for k in sorted(range(1, n_space), key=lambda k: -min(k, n_space - k)):
        remote_copy(
            row_sums.at[place],
            row_sums.at[place],
            stat_send.at[0],
            stat_recv.at[0],
            (slab, lax.rem(place + k, n_space)),
        ).start()
    halo_one = send_halo(raw_one, 0, 2, frames, True, True)

    ids_load.wait()
    own = ids[slab]
    members = [
        jnp.where(ids[lax.rem(slab + n_tm + k - REACH, n_tm)] == own, 1.0, 0.0).astype(F32)
        for k in range(WINDOW)
    ]
    count = functools.reduce(lambda a, b: a + b, members) * frame_count
    starting = jnp.logical_or(slab == 0, ids[before] != own)
    starts = jnp.where(starting, 1.0, 0.0).astype(F32)
    fresh = jnp.full((cols, width), starts, F32) > 0.5
    limits = row_limits(place, n_space, rows)

    wait_for(row_sums.at[pl.ds(0, n_space - 1)], stat_recv.at[0])
    slab_sums[REACH] = jnp.sum(row_sums[...], axis=0)
    for k in (4, 5, 3, 6, 7, 2, 1):
        for offset in (k, -k):
            remote_copy(
                slab_sums.at[REACH],
                slab_sums.at[REACH - offset],
                stat_send.at[1],
                stat_recv.at[1],
                (lax.rem(slab + n_tm + offset, n_tm), place),
            ).start()
    for load in affine_loads:
        load.wait()
    weight_loads[0].wait()
    for copy in halo_one:
        copy.wait_recv()
    wait_for(slab_sums.at[pl.ds(0, WINDOW - 1)], stat_recv.at[1])
    total = jnp.zeros((1, LANES), F32)
    for k in range(WINDOW):
        total = total + slab_sums[k] * members[k]
    mean, scale = unpack_stats(total, count, per_group)
    stats = (mean, scale * affine[0], affine[1])

    halos, hidden_sums = [], [nothing]

    def finish_one(f, value):
        hidden = value.astype(BF16)
        raw_two[f + 2 : f + 4, 1 : rows + 1] = hidden.reshape(2, rows, cols, width)
        hidden_sums[0] = add_up(hidden.astype(F32), hidden_sums[0])
        if f == 2:
            halos.extend(send_halo(raw_two, 1, 4, 2, True, False))

    for f in (2, 3, 4, 5, 0, 1):
        norm_frame(raw_one, act, f, limits, fresh, stats)
    conv_tiles(act, weights_one, ((2, 2), (0, 2)), finish_one)

    all_sums[REACH * n_space + place] = pack_sums(hidden_sums[0], per_group)
    for offset, turn in far_first(n_space):
        remote_copy(
            all_sums.at[REACH * n_space + place],
            all_sums.at[(REACH - offset) * n_space + place],
            stat_send.at[2],
            stat_recv.at[2],
            (lax.rem(slab + n_tm + offset, n_tm), lax.rem(place + turn, n_space)),
        ).start()
    halos.extend(send_halo(raw_two, 2, 2, 2, False, False))
    for copy in halos[:2]:
        copy.wait_recv()
    last, front = pl.ds(frames, 2), pl.ds(0, 2)
    corners = [
        ((last, pl.ds(r, 1)), (front, pl.ds(r, 1)), (after, place)) for r in (0, rows + 1)
    ]
    relayed = start_copies(raw_two, 3, corners)
    table[3:4] = jnp.full((1, width), starts, F32)
    table[2:3] = affine[3]
    weight_loads[1].wait()
    for copy in halos[2:] + relayed:
        copy.wait_recv()
    for copy in halo_one + halos + relayed:
        copy.wait_send()
    wait_for(row_sums.at[pl.ds(0, n_space - 1)], stat_send.at[0])
    wait_for(slab_sums.at[pl.ds(0, WINDOW - 1)], stat_send.at[1])
    others = all_sums.at[pl.ds(0, WINDOW * n_space - 1)]
    wait_for(others, stat_send.at[2])
    wait_for(others, stat_recv.at[2])
    total = jnp.zeros((1, LANES), F32)
    for k in range(WINDOW):
        total = total + jnp.sum(all_sums[pl.ds(k * n_space, n_space)], axis=0) * members[k]
    mean, scale = unpack_stats(total, count, per_group)
    table[0:1] = mean
    table[1:2] = scale * affine[2]


def back_kernel(n_space, feats, raw, weights, table, out, act, result, base, load_sem, out_sem):
    frames, rows, cols, width = feats.shape
    load = local_copy(feats, base, load_sem)
    load.start()
    limits = row_limits(lax.axis_index("space"), n_space, rows)
    stats = (table[0:1], table[1:2], table[2:3])
    fresh = jnp.broadcast_to(table[3:4], (cols, width)) > 0.5
    load.wait()

    stores = []

    def finish_two(f, value):
        count = value.shape[0] // (rows * cols)
        value = value.reshape(count, rows, cols, width)
        result[f : f + count] = value + base[f : f + count].astype(F32)
        span = pl.ds(f, count)
        stores.append(local_copy(result.at[span], out.at[span], out_sem.at[f]))
        stores[-1].start()

    for f in (2, 3, 4, 5, 0, 1):
        norm_frame(raw, act, f, limits, fresh, stats)
    conv_tiles(act, weights, ((3, 1), (2, 1), (1, 1), (0, 1)), finish_two)
    for store in stores:
        store.wait()


def solution(mesh):
    n_tm, n_space = mesh.shape["tm"], mesh.shape["space"]

    def on_device(
        feats, clip_ids, gain_one, shift_one, kernel_one, gain_two, shift_two, kernel_two
    ):
        frames, rows, cols, width = feats.shape
        extended = (frames + 2, rows + 2, cols, width)
        vmem = pltpu.VMEM
        dma = pltpu.SemaphoreType.DMA
        in_hbm = pl.BlockSpec(memory_space=pltpu.HBM)
        in_vmem = pl.BlockSpec(memory_space=pltpu.VMEM)
        row = lambda value: value.reshape(1, width)
        flops = 2 * 27 * frames * rows * cols * width * width
        raw_two, weights_two, table = pl.pallas_call(
            functools.partial(front_kernel, n_tm, n_space),
            out_shape=(
                vmem(extended, BF16),
                vmem(kernel_two.shape, BF16),
                vmem((8, width), F32),
            ),
            in_specs=[in_hbm] * 8,
            out_specs=[in_vmem] * 3,
            scratch_shapes=[
                vmem(extended, BF16),
                vmem(extended, BF16),
                vmem(kernel_one.shape, BF16),
                vmem((4, 1, width), F32),
                pltpu.SMEM((n_tm,), jnp.int32),
                vmem((n_space, 1, LANES), F32),
                vmem((WINDOW, 1, LANES), F32),
                vmem((WINDOW * n_space, 1, LANES), F32),
                dma((frames,)),
                dma((2,)),
                dma((4,)),
                dma,
                dma((3,)),
                dma((3,)),
                dma((4, 5)),
                dma((4, 5)),
            ],
            compiler_params=pltpu.CompilerParams(
                collective_id=0, has_side_effects=True, vmem_limit_bytes=54 << 20
            ),
            cost_estimate=pl.CostEstimate(
                flops=flops, bytes_accessed=8 << 20, transcendentals=0
            ),
            name="front",
        )(
            feats,
            clip_ids,
            row(gain_one),
            row(shift_one),
            kernel_one,
            row(gain_two),
            row(shift_two),
            kernel_two,
        )
        return pl.pallas_call(
            functools.partial(back_kernel, n_space),
            out_shape=jax.ShapeDtypeStruct(feats.shape, F32),
            in_specs=[in_hbm, in_vmem, in_vmem, in_vmem],
            out_specs=in_hbm,
            scratch_shapes=[
                vmem(extended, BF16),
                vmem(feats.shape, F32),
                vmem(feats.shape, BF16),
                dma,
                dma((frames,)),
            ],
            compiler_params=pltpu.CompilerParams(vmem_limit_bytes=24 << 20),
            cost_estimate=pl.CostEstimate(
                flops=flops, bytes_accessed=3 << 20, transcendentals=0
            ),
            name="back",
        )(feats, raw_two, weights_two, table)

    return jax.shard_map(
        on_device,
        mesh=mesh,
        in_specs=(P("tm", "space", None, None), P(), P(), P(), P(), P(), P(), P()),
        out_specs=P("tm", "space", None, None),
        check_vma=False,
    )
```

```python
import functools

import jax
import jax.numpy as jnp
from jax import lax
from jax.experimental import pallas as pl
from jax.experimental.pallas import tpu as pltpu
from jax.sharding import PartitionSpec as P

GROUPS = 32
REACH = 7
WINDOW = 2 * REACH + 1
LANES = 128
MESH = pl.DeviceIdType.MESH
F32 = jnp.float32
BF16 = jnp.bfloat16


def local_copy(src, dst, sem):
    return pltpu.make_async_copy(src, dst, sem)


def remote_copy(src, dst, send_sem, recv_sem, device):
    return pltpu.make_async_remote_copy(
        src_ref=src,
        dst_ref=dst,
        send_sem=send_sem,
        recv_sem=recv_sem,
        device_id=device,
        device_id_type=MESH,
    )


def wait_for(ref, sem):
    pltpu.make_async_copy(ref, ref, sem).wait()


def group_total(value, per_group):
    lane = lax.broadcasted_iota(jnp.int32, value.shape, 1)
    width = value.shape[1]
    step = 1
    while step < per_group:
        upper = pltpu.roll(value, step, 1)
        lower = pltpu.roll(value, width - step, 1)
        value = value + jnp.where((lane & step) != 0, upper, lower)
        step *= 2
    return value


def add_up(value, sums):
    total, square = sums
    value = value.reshape(-1, 8, value.shape[-1])
    return total + jnp.sum(value, axis=0), square + jnp.sum(value * value, axis=0)


def pack_sums(sums, per_group):
    total, square = (jnp.sum(s, axis=0, keepdims=True) for s in sums)
    parts = [
        total[:, :LANES],
        square[:, :LANES],
        total[:, LANES:],
        square[:, LANES:],
    ]
    parts = group_total(jnp.concatenate(parts, axis=0), per_group)
    kind = lax.broadcasted_iota(jnp.int32, (1, LANES), 1) & 3
    packed = parts[3:4]
    for i in range(3):
        packed = jnp.where(kind == i, parts[i : i + 1], packed)
    return packed


def unpack_stats(packed, count, per_group):
    shape = (4, LANES)
    row = lax.broadcasted_iota(jnp.int32, shape, 0)
    lane = lax.broadcasted_iota(jnp.int32, shape, 1)
    spread = jnp.where((lane & (per_group - 1)) == row, jnp.broadcast_to(packed, shape), 0.0)
    total = group_total(spread, per_group) / jnp.full(shape, count, F32)
    mean = jnp.concatenate([total[0:1], total[2:3]], axis=1)
    variance = jnp.concatenate([total[1:2], total[3:4]], axis=1) - mean * mean
    return mean, lax.rsqrt(variance + 1e-06)


def row_limits(place, n_space, rows):
    top = jnp.where(place == 0, 1, 0)
    bottom = jnp.where(place == n_space - 1, rows, rows + 1)
    return top, bottom


def normed(value, mean, factor, shift):
    value = (value - mean) * factor + shift
    return (value / (1.0 + jnp.exp(-value))).astype(BF16)


def norm_frame(raw, act, f, limits, fresh, stats):
    rows = raw.shape[1] - 2
    top, bottom = limits
    for r in range(rows + 2):
        source = top if r == 0 else bottom if r == rows + 1 else r
        value = raw[f, source].astype(F32)
        if f < 2:
            value = jnp.where(fresh, raw[2, source].astype(F32), value)
        act[f, r] = normed(value, *stats)


def tap_sum(act, weights, f, count, l):
    rows, cols, width = act.shape[1] - 2, act.shape[2], act.shape[3]
    total = None
    for i in range(3):
        for j in range(3):
            left = act[f + i : f + i + count, j : j + rows].reshape(count * rows * cols, width)
            term = jnp.dot(left, weights[i, j, l], preferred_element_type=F32)
            total = term if total is None else total + term
    return total


def joined(parts, cols):
    size = parts[0].shape[0]
    col = lax.rem(lax.broadcasted_iota(jnp.int32, parts[0].shape, 0), cols)
    earlier = jnp.where(col == 0, parts[0], pltpu.roll(parts[0], 1, 0))
    later = jnp.where(col == cols - 1, parts[1], pltpu.roll(parts[1], size - 1, 0))
    return parts[2] + (earlier + later)


def conv_tiles(act, weights, tiles, finish):
    cols = act.shape[2]
    waiting = None
    for f, count in tiles:
        parts = [tap_sum(act, weights, f, count, l) for l in (0, 2)]
        if waiting is not None:
            finish(waiting[0], joined(waiting[1], cols))
        parts += [tap_sum(act, weights, f, count, 1)]
        waiting = (f, parts)
    finish(waiting[0], joined(waiting[1], cols))


def far_first(n_space):
    chips = (0.0, 1.0, 2.0, 1.7, 1.0)

    def hops(pair):
        return min(pair[1], n_space - pair[1]) + chips[(abs(pair[0]) + 1) // 2]

    pairs = [(k, d) for k in range(-REACH, REACH + 1) for d in range(n_space) if (k, d) != (0, 0)]
    return sorted(pairs, key=hops, reverse=True)


def front_kernel(
    n_tm,
    n_space,
    feats,
    clip_ids,
    gain_one,
    shift_one,
    kernel_one,
    gain_two,
    shift_two,
    kernel_two,
    raw_two,
    weights_two,
    table,
    raw_one,
    act,
    weights_one,
    affine,
    ids,
    row_sums,
    slab_sums,
    all_sums,
    load_sem,
    weight_sem,
    affine_sem,
    ids_sem,
    stat_send,
    stat_recv,
    halo_send,
    halo_recv,
):
    frames, rows, cols, width = feats.shape
    per_group = width // GROUPS
    slab = lax.axis_index("tm")
    place = lax.axis_index("space")
    after = lax.rem(slab + 1, n_tm)
    before = lax.rem(slab + n_tm - 1, n_tm)
    down = lax.rem(place + 1, n_space)
    up = lax.rem(place + n_space - 1, n_space)

    loads = [
        local_copy(feats.at[f], raw_one.at[f + 2, pl.ds(1, rows)], load_sem.at[f])
        for f in range(frames)
    ]
    for load in loads:
        load.start()

    barrier = pltpu.get_barrier_semaphore()

    def signal(tm, space):
        pl.semaphore_signal(barrier, inc=1, device_id=(tm, space), device_id_type=MESH)

    for k in sorted(range(1, n_space), key=lambda k: -min(k, n_space - k)):
        signal(slab, lax.rem(place + k, n_space))
    for k in (4, 5, 3, 6, 7, 2, 1):
        signal(lax.rem(slab + k, n_tm), place)
        signal(lax.rem(slab + n_tm - k, n_tm), place)
    for tm in (after, before):
        for space in (up, down):
            signal(tm, space)

    ids_load = local_copy(clip_ids, ids, ids_sem)
    ids_load.start()
    affine_loads = [
        local_copy(ref, affine.at[i], affine_sem.at[i])
        for i, ref in enumerate((gain_one, shift_one, gain_two, shift_two))
    ]
    for load in affine_loads:
        load.start()
    weight_loads = [
        local_copy(kernel_one, weights_one, weight_sem.at[0]),
        local_copy(kernel_two, weights_two, weight_sem.at[1]),
    ]

    def send_halo(raw, stage, first, count, ahead, corners):
        span = pl.ds(first, count)
        copies = [
            ((span, pl.ds(1, 1)), (span, pl.ds(rows + 1, 1)), (slab, up)),
            ((span, pl.ds(rows, 1)), (span, pl.ds(0, 1)), (slab, down)),
        ]
        last = pl.ds(frames, 2)
        front = pl.ds(0, 2)
        if ahead:
            copies += [((last, pl.ds(1, rows)), (front, pl.ds(1, rows)), (after, place))]
        if corners:
            copies += [
                ((last, pl.ds(1, 1)), (front, pl.ds(rows + 1, 1)), (after, up)),
                ((last, pl.ds(rows, 1)), (front, pl.ds(0, 1)), (after, down)),
            ]
        return start_copies(raw, stage, copies)

    def start_copies(raw, stage, copies):
        made = []
        for i, (src, dst, device) in enumerate(copies):
            made.append(
                remote_copy(
                    raw.at[src],
                    raw.at[dst],
                    halo_send.at[stage, i],
                    halo_recv.at[stage, i],
                    device,
                )
            )
        for copy in made:
            copy.start()
        return made

    nothing = (jnp.zeros((8, width), F32), jnp.zeros((8, width), F32))
    frame_count = float(frames * rows * n_space * cols * per_group)

    sums = nothing
    for f in range(frames):
        loads[f].wait()
        for r in range(rows):
            sums = add_up(raw_one[f + 2, r + 1].astype(F32), sums)
    for load in weight_loads:
        load.start()
    row_sums[place] = pack_sums(sums, per_group)
    pl.semaphore_wait(barrier, (n_space - 1) + 2 * REACH + 4)
    for k in sorted(range(1, n_space), key=lambda k: -min(k, n_space - k)):
        remote_copy(
            row_sums.at[place],
            row_sums.at[place],
            stat_send.at[0],
            stat_recv.at[0],
            (slab, lax.rem(place + k, n_space)),
        ).start()
    halo_one = send_halo(raw_one, 0, 2, frames, True, True)

    ids_load.wait()
    own = ids[slab]
    members = [
        jnp.where(ids[lax.rem(slab + n_tm + k - REACH, n_tm)] == own, 1.0, 0.0).astype(F32)
        for k in range(WINDOW)
    ]
    count = functools.reduce(lambda a, b: a + b, members) * frame_count
    starting = jnp.logical_or(slab == 0, ids[before] != own)
    starts = jnp.where(starting, 1.0, 0.0).astype(F32)
    fresh = jnp.full((cols, width), starts, F32) > 0.5
    limits = row_limits(place, n_space, rows)

    wait_for(row_sums.at[pl.ds(0, n_space - 1)], stat_recv.at[0])
    slab_sums[REACH] = jnp.sum(row_sums[...], axis=0)
    for k in (4, 5, 3, 6, 7, 2, 1):
        for offset in (k, -k):
            remote_copy(
                slab_sums.at[REACH],
                slab_sums.at[REACH - offset],
                stat_send.at[1],
                stat_recv.at[1],
                (lax.rem(slab + n_tm + offset, n_tm), place),
            ).start()
    for load in affine_loads:
        load.wait()
    weight_loads[0].wait()
    for copy in halo_one:
        copy.wait_recv()
    wait_for(slab_sums.at[pl.ds(0, WINDOW - 1)], stat_recv.at[1])
    total = jnp.zeros((1, LANES), F32)
    for k in range(WINDOW):
        total = total + slab_sums[k] * members[k]
    mean, scale = unpack_stats(total, count, per_group)
    stats = (mean, scale * affine[0], affine[1])

    halos, hidden_sums = [], [nothing]

    def finish_one(f, value):
        hidden = value.astype(BF16)
        raw_two[f + 2 : f + 4, 1 : rows + 1] = hidden.reshape(2, rows, cols, width)
        hidden_sums[0] = add_up(hidden.astype(F32), hidden_sums[0])
        if f == 2:
            halos.extend(send_halo(raw_two, 1, 4, 2, True, False))

    for f in (2, 3, 4, 5, 0, 1):
        norm_frame(raw_one, act, f, limits, fresh, stats)
    conv_tiles(act, weights_one, ((2, 2), (0, 2)), finish_one)

    all_sums[REACH * n_space + place] = pack_sums(hidden_sums[0], per_group)
    for offset, turn in far_first(n_space):
        remote_copy(
            all_sums.at[REACH * n_space + place],
            all_sums.at[(REACH - offset) * n_space + place],
            stat_send.at[2],
            stat_recv.at[2],
            (lax.rem(slab + n_tm + offset, n_tm), lax.rem(place + turn, n_space)),
        ).start()
    halos.extend(send_halo(raw_two, 2, 2, 2, False, False))
    for copy in halos[:2]:
        copy.wait_recv()
    last, front = pl.ds(frames, 2), pl.ds(0, 2)
    corners = [
        ((last, pl.ds(r, 1)), (front, pl.ds(r, 1)), (after, place)) for r in (0, rows + 1)
    ]
    relayed = start_copies(raw_two, 3, corners)
    table[3:4] = jnp.full((1, width), starts, F32)
    table[2:3] = affine[3]
    weight_loads[1].wait()
    for copy in halos[2:] + relayed:
        copy.wait_recv()
    for copy in halo_one + halos + relayed:
        copy.wait_send()
    wait_for(row_sums.at[pl.ds(0, n_space - 1)], stat_send.at[0])
    wait_for(slab_sums.at[pl.ds(0, WINDOW - 1)], stat_send.at[1])
    others = all_sums.at[pl.ds(0, WINDOW * n_space - 1)]
    wait_for(others, stat_send.at[2])
    wait_for(others, stat_recv.at[2])
    total = jnp.zeros((1, LANES), F32)
    for k in range(WINDOW):
        total = total + jnp.sum(all_sums[pl.ds(k * n_space, n_space)], axis=0) * members[k]
    mean, scale = unpack_stats(total, count, per_group)
    table[0:1] = mean
    table[1:2] = scale * affine[2]


def back_kernel(n_space, feats, raw, weights, table, out, act, result, out_sem):
    frames, rows, cols, width = feats.shape
    limits = row_limits(lax.axis_index("space"), n_space, rows)
    stats = (table[0:1], table[1:2], table[2:3])
    fresh = jnp.broadcast_to(table[3:4], (cols, width)) > 0.5

    stores = []

    def finish_two(f, value):
        count = value.shape[0] // (rows * cols)
        value = value.reshape(count, rows, cols, width)
        result[f : f + count] = value + feats[f : f + count].astype(F32)
        span = pl.ds(f, count)
        stores.append(local_copy(result.at[span], out.at[span], out_sem.at[f]))
        stores[-1].start()

    for f in (2, 3, 4, 5, 0, 1):
        norm_frame(raw, act, f, limits, fresh, stats)
    conv_tiles(act, weights, ((2, 2), (1, 1), (0, 1)), finish_two)
    for store in stores:
        store.wait()


def solution(mesh):
    n_tm, n_space = mesh.shape["tm"], mesh.shape["space"]

    def on_device(
        feats, clip_ids, gain_one, shift_one, kernel_one, gain_two, shift_two, kernel_two
    ):
        frames, rows, cols, width = feats.shape
        extended = (frames + 2, rows + 2, cols, width)
        vmem = pltpu.VMEM
        dma = pltpu.SemaphoreType.DMA
        in_hbm = pl.BlockSpec(memory_space=pltpu.HBM)
        in_vmem = pl.BlockSpec(memory_space=pltpu.VMEM)
        row = lambda value: value.reshape(1, width)
        flops = 2 * 27 * frames * rows * cols * width * width
        raw_two, weights_two, table = pl.pallas_call(
            functools.partial(front_kernel, n_tm, n_space),
            out_shape=(
                vmem(extended, BF16),
                vmem(kernel_two.shape, BF16),
                vmem((8, width), F32),
            ),
            in_specs=[in_hbm] * 8,
            out_specs=[in_vmem] * 3,
            scratch_shapes=[
                vmem(extended, BF16),
                vmem(extended, BF16),
                vmem(kernel_one.shape, BF16),
                vmem((4, 1, width), F32),
                pltpu.SMEM((n_tm,), jnp.int32),
                vmem((n_space, 1, LANES), F32),
                vmem((WINDOW, 1, LANES), F32),
                vmem((WINDOW * n_space, 1, LANES), F32),
                dma((frames,)),
                dma((2,)),
                dma((4,)),
                dma,
                dma((3,)),
                dma((3,)),
                dma((4, 5)),
                dma((4, 5)),
            ],
            compiler_params=pltpu.CompilerParams(
                collective_id=0, has_side_effects=True, vmem_limit_bytes=54 << 20
            ),
            cost_estimate=pl.CostEstimate(
                flops=flops, bytes_accessed=8 << 20, transcendentals=0
            ),
            name="front",
        )(
            feats,
            clip_ids,
            row(gain_one),
            row(shift_one),
            kernel_one,
            row(gain_two),
            row(shift_two),
            kernel_two,
        )
        return pl.pallas_call(
            functools.partial(back_kernel, n_space),
            out_shape=jax.ShapeDtypeStruct(feats.shape, F32),
            in_specs=[in_vmem] * 4,
            out_specs=in_hbm,
            scratch_shapes=[
                vmem(extended, BF16),
                vmem(feats.shape, F32),
                dma((frames,)),
            ],
            compiler_params=pltpu.CompilerParams(vmem_limit_bytes=24 << 20),
            cost_estimate=pl.CostEstimate(
                flops=flops, bytes_accessed=3 << 20, transcendentals=0
            ),
            name="back",
        )(feats, raw_two, weights_two, table)

    return jax.shard_map(
        on_device,
        mesh=mesh,
        in_specs=(P("tm", "space", None, None), P(), P(), P(), P(), P(), P(), P()),
        out_specs=P("tm", "space", None, None),
        check_vma=False,
    )
```

```python
import functools

import jax
import jax.numpy as jnp
from jax import lax
from jax.experimental import pallas as pl
from jax.experimental.pallas import tpu as pltpu
from jax.sharding import PartitionSpec as P

GROUPS = 32
REACH = 7
WINDOW = 2 * REACH + 1
LANES = 128
MESH = pl.DeviceIdType.MESH
F32 = jnp.float32
BF16 = jnp.bfloat16


def local_copy(src, dst, sem):
    return pltpu.make_async_copy(src, dst, sem)


def remote_copy(src, dst, send_sem, recv_sem, device):
    return pltpu.make_async_remote_copy(
        src_ref=src,
        dst_ref=dst,
        send_sem=send_sem,
        recv_sem=recv_sem,
        device_id=device,
        device_id_type=MESH,
    )


def wait_for(ref, sem):
    pltpu.make_async_copy(ref, ref, sem).wait()


def group_total(value, per_group):
    lane = lax.broadcasted_iota(jnp.int32, value.shape, 1)
    width = value.shape[1]
    step = 1
    while step < per_group:
        upper = pltpu.roll(value, step, 1)
        lower = pltpu.roll(value, width - step, 1)
        value = value + jnp.where((lane & step) != 0, upper, lower)
        step *= 2
    return value


def add_up(value, sums):
    total, square = sums
    value = value.reshape(-1, 8, value.shape[-1])
    return total + jnp.sum(value, axis=0), square + jnp.sum(value * value, axis=0)


def pack_sums(sums, per_group):
    total, square = (jnp.sum(s, axis=0, keepdims=True) for s in sums)
    parts = [
        total[:, :LANES],
        square[:, :LANES],
        total[:, LANES:],
        square[:, LANES:],
    ]
    parts = group_total(jnp.concatenate(parts, axis=0), per_group)
    kind = lax.broadcasted_iota(jnp.int32, (1, LANES), 1) & 3
    packed = parts[3:4]
    for i in range(3):
        packed = jnp.where(kind == i, parts[i : i + 1], packed)
    return packed


def unpack_stats(packed, count, per_group):
    shape = (4, LANES)
    row = lax.broadcasted_iota(jnp.int32, shape, 0)
    lane = lax.broadcasted_iota(jnp.int32, shape, 1)
    spread = jnp.where((lane & (per_group - 1)) == row, jnp.broadcast_to(packed, shape), 0.0)
    total = group_total(spread, per_group) / jnp.full(shape, count, F32)
    mean = jnp.concatenate([total[0:1], total[2:3]], axis=1)
    variance = jnp.concatenate([total[1:2], total[3:4]], axis=1) - mean * mean
    return mean, lax.rsqrt(variance + 1e-06)


def row_limits(place, n_space, rows):
    top = jnp.where(place == 0, 1, 0)
    bottom = jnp.where(place == n_space - 1, rows, rows + 1)
    return top, bottom


def normed(value, mean, factor, shift):
    value = (value - mean) * factor + shift
    return (value / (1.0 + jnp.exp(-value))).astype(BF16)


def norm_frame(raw, act, f, limits, fresh, stats):
    rows = raw.shape[1] - 2
    top, bottom = limits
    for r in range(rows + 2):
        source = top if r == 0 else bottom if r == rows + 1 else r
        value = raw[f, source].astype(F32)
        if f < 2:
            value = jnp.where(fresh, raw[2, source].astype(F32), value)
        act[f, r] = normed(value, *stats)


def tap_sum(act, weights, f, count, l):
    rows, cols, width = act.shape[1] - 2, act.shape[2], act.shape[3]
    total = None
    for i in range(3):
        for j in range(3):
            left = act[f + i : f + i + count, j : j + rows].reshape(count * rows * cols, width)
            term = jnp.dot(left, weights[i, j, l], preferred_element_type=F32)
            total = term if total is None else total + term
    return total


def joined(parts, cols):
    size = parts[0].shape[0]
    col = lax.rem(lax.broadcasted_iota(jnp.int32, parts[0].shape, 0), cols)
    earlier = jnp.where(col == 0, parts[0], pltpu.roll(parts[0], 1, 0))
    later = jnp.where(col == cols - 1, parts[1], pltpu.roll(parts[1], size - 1, 0))
    return parts[2] + (earlier + later)


def conv_tiles(act, weights, tiles, finish):
    cols = act.shape[2]
    waiting = None
    for f, count in tiles:
        parts = [tap_sum(act, weights, f, count, l) for l in (0, 2)]
        if waiting is not None:
            finish(waiting[0], joined(waiting[1], cols))
        parts += [tap_sum(act, weights, f, count, 1)]
        waiting = (f, parts)
    finish(waiting[0], joined(waiting[1], cols))


def far_first(n_space):
    chips = (0.0, 1.0, 2.0, 1.7, 1.0)

    def hops(pair):
        return min(pair[1], n_space - pair[1]) + chips[(abs(pair[0]) + 1) // 2]

    pairs = [(k, d) for k in range(-REACH, REACH + 1) for d in range(n_space) if (k, d) != (0, 0)]
    return sorted(pairs, key=hops, reverse=True)


def front_kernel(
    n_tm,
    n_space,
    feats,
    clip_ids,
    gain_one,
    shift_one,
    kernel_one,
    gain_two,
    shift_two,
    kernel_two,
    raw_two,
    weights_two,
    table,
    raw_one,
    act,
    weights_one,
    affine,
    ids,
    row_sums,
    slab_sums,
    all_sums,
    load_sem,
    weight_sem,
    affine_sem,
    ids_sem,
    stat_send,
    stat_recv,
    halo_send,
    halo_recv,
):
    frames, rows, cols, width = feats.shape
    per_group = width // GROUPS
    slab = lax.axis_index("tm")
    place = lax.axis_index("space")
    after = lax.rem(slab + 1, n_tm)
    before = lax.rem(slab + n_tm - 1, n_tm)
    down = lax.rem(place + 1, n_space)
    up = lax.rem(place + n_space - 1, n_space)

    loads = [
        local_copy(feats.at[f], raw_one.at[f + 2, pl.ds(1, rows)], load_sem.at[f])
        for f in range(frames)
    ]
    for load in loads:
        load.start()

    barrier = pltpu.get_barrier_semaphore()

    def signal(tm, space):
        pl.semaphore_signal(barrier, inc=1, device_id=(tm, space), device_id_type=MESH)

    for k in sorted(range(1, n_space), key=lambda k: -min(k, n_space - k)):
        signal(slab, lax.rem(place + k, n_space))
    for k in (4, 5, 3, 6, 7, 2, 1):
        signal(lax.rem(slab + k, n_tm), place)
        signal(lax.rem(slab + n_tm - k, n_tm), place)
    for tm in (after, before):
        for space in (up, down):
            signal(tm, space)

    ids_load = local_copy(clip_ids, ids, ids_sem)
    ids_load.start()
    affine_loads = [
        local_copy(ref, affine.at[i], affine_sem.at[i])
        for i, ref in enumerate((gain_one, shift_one, gain_two, shift_two))
    ]
    for load in affine_loads:
        load.start()
    weight_loads = [
        local_copy(kernel_one, weights_one, weight_sem.at[0]),
        local_copy(kernel_two, weights_two, weight_sem.at[1]),
    ]

    def send_halo(raw, stage, first, count, ahead, corners):
        span = pl.ds(first, count)
        copies = [
            ((span, pl.ds(1, 1)), (span, pl.ds(rows + 1, 1)), (slab, up)),
            ((span, pl.ds(rows, 1)), (span, pl.ds(0, 1)), (slab, down)),
        ]
        last = pl.ds(frames, 2)
        front = pl.ds(0, 2)
        if ahead:
            copies += [((last, pl.ds(1, rows)), (front, pl.ds(1, rows)), (after, place))]
        if corners:
            copies += [
                ((last, pl.ds(1, 1)), (front, pl.ds(rows + 1, 1)), (after, up)),
                ((last, pl.ds(rows, 1)), (front, pl.ds(0, 1)), (after, down)),
            ]
        return start_copies(raw, stage, copies)

    def start_copies(raw, stage, copies):
        made = []
        for i, (src, dst, device) in enumerate(copies):
            made.append(
                remote_copy(
                    raw.at[src],
                    raw.at[dst],
                    halo_send.at[stage, i],
                    halo_recv.at[stage, i],
                    device,
                )
            )
        for copy in made:
            copy.start()
        return made

    nothing = (jnp.zeros((8, width), F32), jnp.zeros((8, width), F32))
    frame_count = float(frames * rows * n_space * cols * per_group)

    sums = nothing
    for f in range(frames):
        loads[f].wait()
        for r in range(rows):
            sums = add_up(raw_one[f + 2, r + 1].astype(F32), sums)
    for load in weight_loads:
        load.start()
    row_sums[place] = pack_sums(sums, per_group)
    pl.semaphore_wait(barrier, (n_space - 1) + 2 * REACH + 4)
    for k in sorted(range(1, n_space), key=lambda k: -min(k, n_space - k)):
        remote_copy(
            row_sums.at[place],
            row_sums.at[place],
            stat_send.at[0],
            stat_recv.at[0],
            (slab, lax.rem(place + k, n_space)),
        ).start()
    halo_one = send_halo(raw_one, 0, 2, frames, True, True)

    ids_load.wait()
    own = ids[slab]
    members = [
        jnp.where(ids[lax.rem(slab + n_tm + k - REACH, n_tm)] == own, 1.0, 0.0).astype(F32)
        for k in range(WINDOW)
    ]
    count = functools.reduce(lambda a, b: a + b, members) * frame_count
    starting = jnp.logical_or(slab == 0, ids[before] != own)
    starts = jnp.where(starting, 1.0, 0.0).astype(F32)
    fresh = jnp.full((cols, width), starts, F32) > 0.5
    limits = row_limits(place, n_space, rows)

    wait_for(row_sums.at[pl.ds(0, n_space - 1)], stat_recv.at[0])
    slab_sums[REACH] = jnp.sum(row_sums[...], axis=0)
    for k in (4, 5, 3, 6, 7, 2, 1):
        for offset in (k, -k):
            remote_copy(
                slab_sums.at[REACH],
                slab_sums.at[REACH - offset],
                stat_send.at[1],
                stat_recv.at[1],
                (lax.rem(slab + n_tm + offset, n_tm), place),
            ).start()
    for load in affine_loads:
        load.wait()
    weight_loads[0].wait()
    for copy in halo_one:
        copy.wait_recv()
    wait_for(slab_sums.at[pl.ds(0, WINDOW - 1)], stat_recv.at[1])
    total = jnp.zeros((1, LANES), F32)
    for k in range(WINDOW):
        total = total + slab_sums[k] * members[k]
    mean, scale = unpack_stats(total, count, per_group)
    stats = (mean, scale * affine[0], affine[1])

    halos, hidden_sums = [], [nothing]

    def finish_one(f, value):
        hidden = value.astype(BF16)
        count = value.shape[0] // (rows * cols)
        raw_two[f + 2 : f + 2 + count, 1 : rows + 1] = hidden.reshape(count, rows, cols, width)
        hidden_sums[0] = add_up(hidden.astype(F32), hidden_sums[0])
        if f == 2:
            halos.extend(send_halo(raw_two, 1, 4, 2, True, False))

    for f in (3, 4, 5, 2, 1, 0):
        norm_frame(raw_one, act, f, limits, fresh, stats)
    conv_tiles(act, weights_one, ((3, 1), (2, 1), (0, 2)), finish_one)

    all_sums[REACH * n_space + place] = pack_sums(hidden_sums[0], per_group)
    for offset, turn in far_first(n_space):
        remote_copy(
            all_sums.at[REACH * n_space + place],
            all_sums.at[(REACH - offset) * n_space + place],
            stat_send.at[2],
            stat_recv.at[2],
            (lax.rem(slab + n_tm + offset, n_tm), lax.rem(place + turn, n_space)),
        ).start()
    halos.extend(send_halo(raw_two, 2, 2, 2, False, False))
    for copy in halos[:2]:
        copy.wait_recv()
    last, front = pl.ds(frames, 2), pl.ds(0, 2)
    corners = [
        ((last, pl.ds(r, 1)), (front, pl.ds(r, 1)), (after, place)) for r in (0, rows + 1)
    ]
    relayed = start_copies(raw_two, 3, corners)
    table[3:4] = jnp.full((1, width), starts, F32)
    table[2:3] = affine[3]
    weight_loads[1].wait()
    for copy in halos[2:] + relayed:
        copy.wait_recv()
    for copy in halo_one + halos + relayed:
        copy.wait_send()
    wait_for(row_sums.at[pl.ds(0, n_space - 1)], stat_send.at[0])
    wait_for(slab_sums.at[pl.ds(0, WINDOW - 1)], stat_send.at[1])
    others = all_sums.at[pl.ds(0, WINDOW * n_space - 1)]
    wait_for(others, stat_send.at[2])
    wait_for(others, stat_recv.at[2])
    total = jnp.zeros((1, LANES), F32)
    for k in range(WINDOW):
        total = total + jnp.sum(all_sums[pl.ds(k * n_space, n_space)], axis=0) * members[k]
    mean, scale = unpack_stats(total, count, per_group)
    table[0:1] = mean
    table[1:2] = scale * affine[2]


def back_kernel(n_space, feats, raw, weights, table, out, act, result, out_sem):
    frames, rows, cols, width = feats.shape
    limits = row_limits(lax.axis_index("space"), n_space, rows)
    stats = (table[0:1], table[1:2], table[2:3])
    fresh = jnp.broadcast_to(table[3:4], (cols, width)) > 0.5

    stores = []

    def finish_two(f, value):
        count = value.shape[0] // (rows * cols)
        value = value.reshape(count, rows, cols, width)
        result[f : f + count] = value + feats[f : f + count].astype(F32)
        span = pl.ds(f, count)
        stores.append(local_copy(result.at[span], out.at[span], out_sem.at[f]))
        stores[-1].start()

    for f in (2, 3, 4, 5, 0, 1):
        norm_frame(raw, act, f, limits, fresh, stats)
    conv_tiles(act, weights, ((2, 2), (1, 1), (0, 1)), finish_two)
    for store in stores:
        store.wait()


def solution(mesh):
    n_tm, n_space = mesh.shape["tm"], mesh.shape["space"]

    def on_device(
        feats, clip_ids, gain_one, shift_one, kernel_one, gain_two, shift_two, kernel_two
    ):
        frames, rows, cols, width = feats.shape
        extended = (frames + 2, rows + 2, cols, width)
        vmem = pltpu.VMEM
        dma = pltpu.SemaphoreType.DMA
        in_hbm = pl.BlockSpec(memory_space=pltpu.HBM)
        in_vmem = pl.BlockSpec(memory_space=pltpu.VMEM)
        row = lambda value: value.reshape(1, width)
        flops = 2 * 27 * frames * rows * cols * width * width
        raw_two, weights_two, table = pl.pallas_call(
            functools.partial(front_kernel, n_tm, n_space),
            out_shape=(
                vmem(extended, BF16),
                vmem(kernel_two.shape, BF16),
                vmem((8, width), F32),
            ),
            in_specs=[in_hbm] * 8,
            out_specs=[in_vmem] * 3,
            scratch_shapes=[
                vmem(extended, BF16),
                vmem(extended, BF16),
                vmem(kernel_one.shape, BF16),
                vmem((4, 1, width), F32),
                pltpu.SMEM((n_tm,), jnp.int32),
                vmem((n_space, 1, LANES), F32),
                vmem((WINDOW, 1, LANES), F32),
                vmem((WINDOW * n_space, 1, LANES), F32),
                dma((frames,)),
                dma((2,)),
                dma((4,)),
                dma,
                dma((3,)),
                dma((3,)),
                dma((4, 5)),
                dma((4, 5)),
            ],
            compiler_params=pltpu.CompilerParams(
                collective_id=0, has_side_effects=True, vmem_limit_bytes=54 << 20
            ),
            cost_estimate=pl.CostEstimate(
                flops=flops, bytes_accessed=8 << 20, transcendentals=0
            ),
            name="front",
        )(
            feats,
            clip_ids,
            row(gain_one),
            row(shift_one),
            kernel_one,
            row(gain_two),
            row(shift_two),
            kernel_two,
        )
        return pl.pallas_call(
            functools.partial(back_kernel, n_space),
            out_shape=jax.ShapeDtypeStruct(feats.shape, F32),
            in_specs=[in_vmem] * 4,
            out_specs=in_hbm,
            scratch_shapes=[
                vmem(extended, BF16),
                vmem(feats.shape, F32),
                dma((frames,)),
            ],
            compiler_params=pltpu.CompilerParams(vmem_limit_bytes=24 << 20),
            cost_estimate=pl.CostEstimate(
                flops=flops, bytes_accessed=3 << 20, transcendentals=0
            ),
            name="back",
        )(feats, raw_two, weights_two, table)

    return jax.shard_map(
        on_device,
        mesh=mesh,
        in_specs=(P("tm", "space", None, None), P(), P(), P(), P(), P(), P(), P()),
        out_specs=P("tm", "space", None, None),
        check_vma=False,
    )
```

```python
import functools

import jax
import jax.numpy as jnp
from jax import lax
from jax.experimental import pallas as pl
from jax.experimental.pallas import tpu as pltpu
from jax.sharding import PartitionSpec as P

GROUPS = 32
REACH = 7
WINDOW = 2 * REACH + 1
LANES = 128
MESH = pl.DeviceIdType.MESH
F32 = jnp.float32
BF16 = jnp.bfloat16


def local_copy(src, dst, sem):
    return pltpu.make_async_copy(src, dst, sem)


def remote_copy(src, dst, send_sem, recv_sem, device):
    return pltpu.make_async_remote_copy(
        src_ref=src,
        dst_ref=dst,
        send_sem=send_sem,
        recv_sem=recv_sem,
        device_id=device,
        device_id_type=MESH,
    )


def wait_for(ref, sem):
    pltpu.make_async_copy(ref, ref, sem).wait()


def group_total(value, per_group):
    lane = lax.broadcasted_iota(jnp.int32, value.shape, 1)
    width = value.shape[1]
    step = 1
    while step < per_group:
        upper = pltpu.roll(value, step, 1)
        lower = pltpu.roll(value, width - step, 1)
        value = value + jnp.where((lane & step) != 0, upper, lower)
        step *= 2
    return value


def add_up(value, sums):
    total, square = sums
    value = value.reshape(-1, 8, value.shape[-1])
    return total + jnp.sum(value, axis=0), square + jnp.sum(value * value, axis=0)


def pack_sums(sums):
    total, square = sums
    shape = (total.shape[0], LANES)
    lane = lax.broadcasted_iota(jnp.int32, shape, 1)

    def merged(low, high, step):
        is_high = (lane & step) != 0
        beside = jnp.where(is_high, pltpu.roll(high, step, 1), pltpu.roll(low, LANES - step, 1))
        return jnp.where(is_high, high, low) + beside

    low = merged(total[:, :LANES], square[:, :LANES], 1)
    high = merged(total[:, LANES:], square[:, LANES:], 1)
    packed = merged(low, high, 2)
    return jnp.sum(merged(packed, packed, 4), axis=0, keepdims=True)


def unpack_stats(packed, count, per_group):
    shape = (4, LANES)
    row = lax.broadcasted_iota(jnp.int32, shape, 0)
    lane = lax.broadcasted_iota(jnp.int32, shape, 1)
    spread = jnp.where((lane & (per_group - 1)) == row, jnp.broadcast_to(packed, shape), 0.0)
    total = group_total(spread, per_group) / jnp.full(shape, count, F32)
    mean = jnp.concatenate([total[0:1], total[2:3]], axis=1)
    variance = jnp.concatenate([total[1:2], total[3:4]], axis=1) - mean * mean
    return mean, lax.rsqrt(variance + 1e-06)


def row_limits(place, n_space, rows):
    top = jnp.where(place == 0, 1, 0)
    bottom = jnp.where(place == n_space - 1, rows, rows + 1)
    return top, bottom


def normed(value, mean, factor, shift):
    value = (value - mean) * factor + shift
    return (value / (1.0 + jnp.exp(-value))).astype(BF16)


def norm_frame(raw, act, f, limits, fresh, stats):
    rows = raw.shape[1] - 2
    top, bottom = limits
    for r in range(rows + 2):
        source = top if r == 0 else bottom if r == rows + 1 else r
        value = raw[f, source].astype(F32)
        if f < 2:
            value = jnp.where(fresh, raw[2, source].astype(F32), value)
        act[f, r] = normed(value, *stats)


def tap_sum(act, weights, f, count, l):
    rows, cols, width = act.shape[1] - 2, act.shape[2], act.shape[3]
    total = None
    for i in range(3):
        for j in range(3):
            left = act[f + i : f + i + count, j : j + rows].reshape(count * rows * cols, width)
            term = jnp.dot(left, weights[i, j, l], preferred_element_type=F32)
            total = term if total is None else total + term
    return total


def joined(parts, cols):
    size = parts[0].shape[0]
    col = lax.rem(lax.broadcasted_iota(jnp.int32, parts[0].shape, 0), cols)
    earlier = jnp.where(col == 0, parts[0], pltpu.roll(parts[0], 1, 0))
    later = jnp.where(col == cols - 1, parts[1], pltpu.roll(parts[1], size - 1, 0))
    return parts[2] + (earlier + later)


def conv_tiles(act, weights, tiles, finish):
    cols = act.shape[2]
    waiting = None
    for f, count in tiles:
        parts = [tap_sum(act, weights, f, count, l) for l in (0, 2)]
        if waiting is not None:
            finish(waiting[0], joined(waiting[1], cols))
        parts += [tap_sum(act, weights, f, count, 1)]
        waiting = (f, parts)
    finish(waiting[0], joined(waiting[1], cols))


def far_first(n_space):
    chips = (0.0, 1.0, 2.0, 1.7, 1.0)

    def hops(pair):
        return min(pair[1], n_space - pair[1]) + chips[(abs(pair[0]) + 1) // 2]

    pairs = [(k, d) for k in range(-REACH, REACH + 1) for d in range(n_space) if (k, d) != (0, 0)]
    return sorted(pairs, key=hops, reverse=True)


def front_kernel(
    n_tm,
    n_space,
    feats,
    clip_ids,
    gain_one,
    shift_one,
    kernel_one,
    gain_two,
    shift_two,
    kernel_two,
    raw_two,
    weights_two,
    table,
    raw_one,
    act,
    weights_one,
    affine,
    ids,
    row_sums,
    slab_sums,
    all_sums,
    load_sem,
    weight_sem,
    affine_sem,
    ids_sem,
    stat_send,
    stat_recv,
    halo_send,
    halo_recv,
):
    frames, rows, cols, width = feats.shape
    per_group = width // GROUPS
    slab = lax.axis_index("tm")
    place = lax.axis_index("space")
    after = lax.rem(slab + 1, n_tm)
    before = lax.rem(slab + n_tm - 1, n_tm)
    down = lax.rem(place + 1, n_space)
    up = lax.rem(place + n_space - 1, n_space)

    loads = [
        local_copy(feats.at[f], raw_one.at[f + 2, pl.ds(1, rows)], load_sem.at[f])
        for f in range(frames)
    ]
    for load in loads:
        load.start()

    barrier = pltpu.get_barrier_semaphore()

    def signal(tm, space):
        pl.semaphore_signal(barrier, inc=1, device_id=(tm, space), device_id_type=MESH)

    for k in sorted(range(1, n_space), key=lambda k: -min(k, n_space - k)):
        signal(slab, lax.rem(place + k, n_space))
    for k in (4, 5, 3, 6, 7, 2, 1):
        signal(lax.rem(slab + k, n_tm), place)
        signal(lax.rem(slab + n_tm - k, n_tm), place)
    for tm in (after, before):
        for space in (up, down):
            signal(tm, space)

    ids_load = local_copy(clip_ids, ids, ids_sem)
    ids_load.start()
    affine_loads = [
        local_copy(ref, affine.at[i], affine_sem.at[i])
        for i, ref in enumerate((gain_one, shift_one, gain_two, shift_two))
    ]
    for load in affine_loads:
        load.start()
    weight_loads = [
        local_copy(kernel_one, weights_one, weight_sem.at[0]),
        local_copy(kernel_two, weights_two, weight_sem.at[1]),
    ]

    def send_halo(raw, stage, first, count, ahead, corners):
        span = pl.ds(first, count)
        copies = [
            ((span, pl.ds(1, 1)), (span, pl.ds(rows + 1, 1)), (slab, up)),
            ((span, pl.ds(rows, 1)), (span, pl.ds(0, 1)), (slab, down)),
        ]
        last = pl.ds(frames, 2)
        front = pl.ds(0, 2)
        if ahead:
            copies += [((last, pl.ds(1, rows)), (front, pl.ds(1, rows)), (after, place))]
        if corners:
            copies += [
                ((last, pl.ds(1, 1)), (front, pl.ds(rows + 1, 1)), (after, up)),
                ((last, pl.ds(rows, 1)), (front, pl.ds(0, 1)), (after, down)),
            ]
        return start_copies(raw, stage, copies)

    def start_copies(raw, stage, copies):
        made = []
        for i, (src, dst, device) in enumerate(copies):
            made.append(
                remote_copy(
                    raw.at[src],
                    raw.at[dst],
                    halo_send.at[stage, i],
                    halo_recv.at[stage, i],
                    device,
                )
            )
        for copy in made:
            copy.start()
        return made

    nothing = (jnp.zeros((8, width), F32), jnp.zeros((8, width), F32))
    frame_count = float(frames * rows * n_space * cols * per_group)

    sums = nothing
    for f in range(frames):
        loads[f].wait()
        for r in range(rows):
            sums = add_up(raw_one[f + 2, r + 1].astype(F32), sums)
    for load in weight_loads:
        load.start()
    row_sums[place] = pack_sums(sums)
    pl.semaphore_wait(barrier, (n_space - 1) + 2 * REACH + 4)
    for k in sorted(range(1, n_space), key=lambda k: -min(k, n_space - k)):
        remote_copy(
            row_sums.at[place],
            row_sums.at[place],
            stat_send.at[0],
            stat_recv.at[0],
            (slab, lax.rem(place + k, n_space)),
        ).start()
    halo_one = send_halo(raw_one, 0, 2, frames, True, True)

    ids_load.wait()
    own = ids[slab]
    members = [
        jnp.where(ids[lax.rem(slab + n_tm + k - REACH, n_tm)] == own, 1.0, 0.0).astype(F32)
        for k in range(WINDOW)
    ]
    count = functools.reduce(lambda a, b: a + b, members) * frame_count
    starting = jnp.logical_or(slab == 0, ids[before] != own)
    starts = jnp.where(starting, 1.0, 0.0).astype(F32)
    fresh = jnp.full((cols, width), starts, F32) > 0.5
    limits = row_limits(place, n_space, rows)

    wait_for(row_sums.at[pl.ds(0, n_space - 1)], stat_recv.at[0])
    slab_sums[REACH] = jnp.sum(row_sums[...], axis=0)
    for k in (4, 5, 3, 6, 7, 2, 1):
        for offset in (k, -k):
            remote_copy(
                slab_sums.at[REACH],
                slab_sums.at[REACH - offset],
                stat_send.at[1],
                stat_recv.at[1],
                (lax.rem(slab + n_tm + offset, n_tm), place),
            ).start()
    for load in affine_loads:
        load.wait()
    weight_loads[0].wait()
    for copy in halo_one:
        copy.wait_recv()
    wait_for(slab_sums.at[pl.ds(0, WINDOW - 1)], stat_recv.at[1])
    total = jnp.zeros((1, LANES), F32)
    for k in range(WINDOW):
        total = total + slab_sums[k] * members[k]
    mean, scale = unpack_stats(total, count, per_group)
    stats = (mean, scale * affine[0], affine[1])

    halos, hidden_sums = [], [nothing]

    def finish_one(f, value):
        hidden = value.astype(BF16)
        count = value.shape[0] // (rows * cols)
        raw_two[f + 2 : f + 2 + count, 1 : rows + 1] = hidden.reshape(count, rows, cols, width)
        hidden_sums[0] = add_up(hidden.astype(F32), hidden_sums[0])
        if f == 2:
            halos.extend(send_halo(raw_two, 1, 4, 2, True, False))

    for f in (3, 4, 5, 2, 1, 0):
        norm_frame(raw_one, act, f, limits, fresh, stats)
    conv_tiles(act, weights_one, ((3, 1), (2, 1), (0, 2)), finish_one)

    all_sums[REACH * n_space + place] = pack_sums(hidden_sums[0])
    for offset, turn in far_first(n_space):
        remote_copy(
            all_sums.at[REACH * n_space + place],
            all_sums.at[(REACH - offset) * n_space + place],
            stat_send.at[2],
            stat_recv.at[2],
            (lax.rem(slab + n_tm + offset, n_tm), lax.rem(place + turn, n_space)),
        ).start()
    halos.extend(send_halo(raw_two, 2, 2, 2, False, False))
    for copy in halos[:2]:
        copy.wait_recv()
    last, front = pl.ds(frames, 2), pl.ds(0, 2)
    corners = [
        ((last, pl.ds(r, 1)), (front, pl.ds(r, 1)), (after, place)) for r in (0, rows + 1)
    ]
    relayed = start_copies(raw_two, 3, corners)
    table[3:4] = jnp.full((1, width), starts, F32)
    table[2:3] = affine[3]
    weight_loads[1].wait()
    for copy in halos[2:] + relayed:
        copy.wait_recv()
    for copy in halo_one + halos + relayed:
        copy.wait_send()
    wait_for(row_sums.at[pl.ds(0, n_space - 1)], stat_send.at[0])
    wait_for(slab_sums.at[pl.ds(0, WINDOW - 1)], stat_send.at[1])
    others = all_sums.at[pl.ds(0, WINDOW * n_space - 1)]
    wait_for(others, stat_send.at[2])
    wait_for(others, stat_recv.at[2])
    total = jnp.zeros((1, LANES), F32)
    for k in range(WINDOW):
        total = total + jnp.sum(all_sums[pl.ds(k * n_space, n_space)], axis=0) * members[k]
    mean, scale = unpack_stats(total, count, per_group)
    table[0:1] = mean
    table[1:2] = scale * affine[2]


def back_kernel(n_space, feats, raw, weights, table, out, act, result, out_sem):
    frames, rows, cols, width = feats.shape
    limits = row_limits(lax.axis_index("space"), n_space, rows)
    stats = (table[0:1], table[1:2], table[2:3])
    fresh = jnp.broadcast_to(table[3:4], (cols, width)) > 0.5

    stores = []

    def finish_two(f, value):
        count = value.shape[0] // (rows * cols)
        value = value.reshape(count, rows, cols, width)
        result[f : f + count] = value + feats[f : f + count].astype(F32)
        span = pl.ds(f, count)
        stores.append(local_copy(result.at[span], out.at[span], out_sem.at[f]))
        stores[-1].start()

    for f in (2, 3, 4, 5, 0, 1):
        norm_frame(raw, act, f, limits, fresh, stats)
    conv_tiles(act, weights, ((2, 2), (1, 1), (0, 1)), finish_two)
    for store in stores:
        store.wait()


def solution(mesh):
    n_tm, n_space = mesh.shape["tm"], mesh.shape["space"]

    def on_device(
        feats, clip_ids, gain_one, shift_one, kernel_one, gain_two, shift_two, kernel_two
    ):
        frames, rows, cols, width = feats.shape
        extended = (frames + 2, rows + 2, cols, width)
        vmem = pltpu.VMEM
        dma = pltpu.SemaphoreType.DMA
        in_hbm = pl.BlockSpec(memory_space=pltpu.HBM)
        in_vmem = pl.BlockSpec(memory_space=pltpu.VMEM)
        row = lambda value: value.reshape(1, width)
        flops = 2 * 27 * frames * rows * cols * width * width
        raw_two, weights_two, table = pl.pallas_call(
            functools.partial(front_kernel, n_tm, n_space),
            out_shape=(
                vmem(extended, BF16),
                vmem(kernel_two.shape, BF16),
                vmem((8, width), F32),
            ),
            in_specs=[in_hbm] * 8,
            out_specs=[in_vmem] * 3,
            scratch_shapes=[
                vmem(extended, BF16),
                vmem(extended, BF16),
                vmem(kernel_one.shape, BF16),
                vmem((4, 1, width), F32),
                pltpu.SMEM((n_tm,), jnp.int32),
                vmem((n_space, 1, LANES), F32),
                vmem((WINDOW, 1, LANES), F32),
                vmem((WINDOW * n_space, 1, LANES), F32),
                dma((frames,)),
                dma((2,)),
                dma((4,)),
                dma,
                dma((3,)),
                dma((3,)),
                dma((4, 5)),
                dma((4, 5)),
            ],
            compiler_params=pltpu.CompilerParams(
                collective_id=0, has_side_effects=True, vmem_limit_bytes=54 << 20
            ),
            cost_estimate=pl.CostEstimate(
                flops=flops, bytes_accessed=8 << 20, transcendentals=0
            ),
            name="front",
        )(
            feats,
            clip_ids,
            row(gain_one),
            row(shift_one),
            kernel_one,
            row(gain_two),
            row(shift_two),
            kernel_two,
        )
        return pl.pallas_call(
            functools.partial(back_kernel, n_space),
            out_shape=jax.ShapeDtypeStruct(feats.shape, F32),
            in_specs=[in_vmem] * 4,
            out_specs=in_hbm,
            scratch_shapes=[
                vmem(extended, BF16),
                vmem(feats.shape, F32),
                dma((frames,)),
            ],
            compiler_params=pltpu.CompilerParams(vmem_limit_bytes=24 << 20),
            cost_estimate=pl.CostEstimate(
                flops=flops, bytes_accessed=3 << 20, transcendentals=0
            ),
            name="back",
        )(feats, raw_two, weights_two, table)

    return jax.shard_map(
        on_device,
        mesh=mesh,
        in_specs=(P("tm", "space", None, None), P(), P(), P(), P(), P(), P(), P()),
        out_specs=P("tm", "space", None, None),
        check_vma=False,
    )
```
